32 devices in a mesh: pipe: 2 (over x), expert: 16 (over z, y, core).
Axes of the slice: x: 2, y: 2, z: 4, core: 2. Of those that a mesh axis runs over, the one named last changes fastest.
Arguments:
- front_tokens: bfloat16 [2, 192, 3584], P('pipe', 'expert'), may hold values from -6 to 6
- front_routes: int32 [2, 192, 2], P('pipe', 'expert'), may hold values from 0 to 1, all different within a row; in each aligned block of 12 rows (0 to 11, 12 to 23, ..., all dimensions but the last counted through in order) at most 12 rows name the same one
- front_mixing: int32 [2, 192, 2], P('pipe', 'expert'), may hold values from 1 to 15
- back_tokens: bfloat16 [2, 192, 3584], P('pipe', 'expert'), may hold values from -6 to 6
- back_routes: int32 [2, 192, 2], P('pipe', 'expert'), may hold values from 0 to 1, all different within a row; in each aligned block of 12 rows (0 to 11, 12 to 23, ..., all dimensions but the last counted through in order) at most 12 rows name the same one
- back_mixing: int32 [2, 192, 2], P('pipe', 'expert'), may hold values from 1 to 15
- back_upstream: bfloat16 [2, 192, 3584], P('pipe', 'expert'), may hold values from -6 to 6
- gate_weight: bfloat16 [2, 3584, 2048], P('pipe', None, 'expert'), may hold values from -0.09375 to 0.09375
- up_weight: bfloat16 [2, 3584, 2048], P('pipe', None, 'expert'), may hold values from -0.09375 to 0.09375
- down_weight: bfloat16 [2, 2048, 3584], P('pipe', 'expert'), may hold values from -0.1875 to 0.1875
Outputs:
- front_result: bfloat16 [2, 192, 3584], P('pipe', 'expert')
- token_grads: bfloat16 [2, 192, 3584], P('pipe', 'expert')
- gate_grads: bfloat16 [2, 1792, 2048], P('pipe', None, 'expert')
- up_grads: bfloat16 [2, 1792, 2048], P('pipe', None, 'expert')
- down_grads: bfloat16 [2, 2048, 1792], P('pipe', 'expert')
The draws below stay inside these ranges and needn't reach their ends.
Inputs may be any that keep to these rules, and one draw needn't show every extreme that they name: `front_routes`: each row names 2 different experts; within each device's block of 12 rows no expert is named more than 12 times, a bound that some block reaches. `back_routes`: each row names 2 different experts; within each device's block of 12 rows no expert is named more than 12 times, a bound that some block reaches.
All inputs are finite; a program needn't handle non-finite values.
Results may differ from the reference program's by a relative error of at most 0.0071.
Values may be sent and summed in bfloat16 or wider, within the bound.
A program may use at most 64 MiB of HBM per device.

```python
import math
import jax
import jax.numpy as jnp
import numpy as np
from jax import lax

D = 3584
FFW = 1024
SHARDS = 8
FFD = 128
TOP = 2
TOK_DEV = 12
EXPERTS = 2
CAP = 12
TOKENS = 192
N_PIPE = 2
N_EXPERT = 16


def touch_ends(entries, own_key, low, top_value):
    longest = entries.shape.index(max(entries.shape))
    spots = []
    for shift in (0, 1):
        where = [jax.random.randint(jax.random.fold_in(own_key, axis), (), 0, length) for axis, length in enumerate(entries.shape)]
        where[longest] = (where[longest] + shift) % entries.shape[longest]
        spots.append(tuple(where))
    return entries.at[spots[0]].set(low).at[spots[1]].set(top_value)


def level_of(rng, dims, split, low, high):
    gain = 1.0
    for axis_at, blocks in split:
        steps = jax.random.uniform(jax.random.fold_in(jax.random.fold_in(rng, 6), axis_at), (blocks,), jnp.float32, low / len(split), high / len(split))
        gain = gain * jnp.repeat(jnp.exp(steps), dims[axis_at] // blocks).reshape((-1,) + (1,) * (len(dims) - 1 - axis_at))
    return gain


def routed_block(key, own, number, rows, number_of, top, bound, lean):
    order = jax.random.permutation(key, number_of)
    packed, usual = load_shares(number_of, rows * top, bound, lean, True), load_shares(number_of, rows * top, bound, lean, False)
    places = jnp.arange(number_of)

    def named(lengths, offset_by):
        used = int((lengths > 0).sum())
        fixed = max(1, used // 4)
        shifted = fixed + (places - fixed + offset_by * (used - fixed)) % max(1, number_of - fixed)
        return jnp.zeros((number_of,), jnp.int32).at[order[jnp.where(places < fixed, places, shifted)]].set(jnp.asarray(lengths, jnp.int32))

    lengths = jnp.where(number % 4 == 0, named(packed, number // 4), named(usual, number - number // 4 - 1))
    mixed = jax.random.permutation(jax.random.fold_in(own, 3), number_of)
    donor, taker = mixed[0:number_of // 2 * 2:2], mixed[1:number_of // 2 * 2:2]
    margin = jnp.minimum(lengths[donor] - 1, bound - lengths[taker]) // 2
    margin = jnp.where((donor == order[0]) | (taker == order[0]) | (lengths[taker] == 0), 0, jnp.maximum(margin, 0))
    shifted = jax.random.randint(jax.random.fold_in(own, 4), (number_of // 2,), 0, 1 << 20) % (margin + 1)
    lengths = lengths.at[donor].add(-shifted).at[taker].add(shifted)
    items = jnp.searchsorted(jnp.cumsum(lengths), jnp.arange(rows * top), side="right").astype(jnp.int32)
    table = items.reshape(top, rows).T
    table = table[jax.random.permutation(jax.random.fold_in(own, 1), rows)]
    offset_by = jax.random.randint(jax.random.fold_in(own, 2), (rows, 1), 0, top)
    return jnp.take_along_axis(table, (jnp.arange(top)[None, :] + offset_by) % top, axis=1)


def load_shares(count, total, bound, skew, full):
    weights = [(1 << 20) // math.isqrt(grade ** skew) + 1 for grade in range(1, count + 1)]
    largest = bound if full else min(bound, max(-(-total // count), total * weights[0] // sum(weights)))
    least = 1 if total - largest >= count - 1 else 0
    given, surplus = [largest] + [least] * (count - 1), total - largest - least * (count - 1)
    while surplus > 0:
        candidates = [i for i in range(1, count) if given[i] < largest] or [i for i in range(1, count) if given[i] < bound]
        whole, left = sum([weights[i] for i in candidates]), surplus
        for i in candidates:
            extra = min(bound - given[i], max(1, left * weights[i] // whole), surplus)
            given[i] = given[i] + extra
            surplus = surplus - extra
    return np.array(given)


def normal_values(stream_key, dims, scale, bound, cuts=(), held_as=jnp.bfloat16):
    factor_of = level_of(stream_key, dims, cuts, -0.22, 0.18) if cuts else 1.0
    result = jax.random.normal(stream_key, dims, jnp.float32) * scale * factor_of
    return jnp.minimum(jnp.maximum(result, -bound), bound).astype(held_as)


def setup_inputs(seed: int = 0) -> dict:
    arg_keys = jax.random.split(jax.random.key(seed), 11)
    front_tokens = normal_values(arg_keys[0], (N_PIPE, TOKENS, D), 1.0, 6.0, ((0, 2), (1, 16)))
    front_routes_keys = jax.random.split(jax.random.fold_in(arg_keys[1], 1), N_PIPE * TOKENS // TOK_DEV)
    front_routes_turns = jax.random.permutation(jax.random.fold_in(arg_keys[1], 3), N_PIPE * TOKENS // TOK_DEV)
    front_routes = jax.vmap(lambda own, number: routed_block(jax.random.fold_in(arg_keys[1], 2), own, number, TOK_DEV, EXPERTS, TOP, CAP, 0))(front_routes_keys, front_routes_turns).reshape((N_PIPE, TOKENS, TOP))
    front_mixing = touch_ends(jax.random.randint(arg_keys[2], (N_PIPE, TOKENS, TOP), 1, 16), jax.random.fold_in(arg_keys[2], 1), 1, 15).astype(jnp.int32)
    back_tokens = normal_values(arg_keys[3], (N_PIPE, TOKENS, D), 1.0, 6.0, ((0, 2), (1, 16)))
    back_routes_keys = jax.random.split(jax.random.fold_in(arg_keys[4], 1), N_PIPE * TOKENS // TOK_DEV)
    back_routes_turns = jax.random.permutation(jax.random.fold_in(arg_keys[4], 3), N_PIPE * TOKENS // TOK_DEV)
    back_routes = jax.vmap(lambda own, number: routed_block(jax.random.fold_in(arg_keys[4], 2), own, number, TOK_DEV, EXPERTS, TOP, CAP, 0))(back_routes_keys, back_routes_turns).reshape((N_PIPE, TOKENS, TOP))
    back_mixing = touch_ends(jax.random.randint(arg_keys[5], (N_PIPE, TOKENS, TOP), 1, 16), jax.random.fold_in(arg_keys[5], 1), 1, 15).astype(jnp.int32)
    back_upstream = normal_values(arg_keys[6], (N_PIPE, TOKENS, D), 1.0, 6.0, ((0, 2), (1, 16)))
    gate_weight = normal_values(arg_keys[7], (N_PIPE, D, EXPERTS * FFW), D ** -0.5, 0.09375, ((0, 2), (2, 16)))
    up_weight = normal_values(arg_keys[8], (N_PIPE, D, EXPERTS * FFW), D ** -0.5, 0.09375, ((0, 2), (2, 16)))
    down_weight = normal_values(arg_keys[9], (N_PIPE, EXPERTS * FFW, D), FFW ** -0.5, 0.1875, ((0, 2), (1, 16)))
    return {"front_tokens": front_tokens, "front_routes": front_routes, "front_mixing": front_mixing, "back_tokens": back_tokens, "back_routes": back_routes, "back_mixing": back_mixing, "back_upstream": back_upstream, "gate_weight": gate_weight, "up_weight": up_weight, "down_weight": down_weight}


weight_unit = 0.0625


def slot_table(routes):
    per_block = routes.reshape(N_EXPERT, TOK_DEV * TOP)
    matches = (per_block[:, :, None] == jnp.arange(EXPERTS, dtype=jnp.int32)[None, None, :]).astype(jnp.int32)
    earlier = jnp.cumsum(matches, axis=1) - matches
    position = jnp.sum(earlier * matches, axis=2)
    blocks = jnp.arange(N_EXPERT, dtype=jnp.int32)[:, None]
    return (blocks * CAP + position).reshape(TOKENS, TOP).astype(jnp.int32)


def scatter_rows(values, routes, slot_index):
    buffer = jnp.zeros((EXPERTS, N_EXPERT * CAP, D), values.dtype)
    return buffer.at[routes, slot_index].set(values)


def barrier_float(values):
    return lax.optimization_barrier(values).astype(jnp.float32)


def shard_total(shard_parts):
    return jnp.sum(barrier_float(shard_parts.astype(jnp.bfloat16)), axis=0).astype(jnp.bfloat16)


def forward_expert(operands):
    tok_rows, gate_cols, up_cols, down_rows = operands
    gate_val = jnp.dot(tok_rows, gate_cols, preferred_element_type=jnp.float32)
    up_val = jnp.dot(tok_rows, up_cols, preferred_element_type=jnp.float32)
    hidden = (jax.nn.silu(gate_val) * up_val).astype(jnp.bfloat16)
    split_hidden = barrier_float(hidden).reshape(-1, SHARDS, FFD)
    split_down = down_rows.astype(jnp.float32).reshape(SHARDS, FFD, D)
    shard_parts = jnp.einsum("rsf,sfd->srd", split_hidden, split_down)
    return shard_total(shard_parts)


def backward_expert(operands):
    tok_rows, scaled_rows, gate_cols, up_cols, down_rows = operands
    gate_val = jnp.dot(tok_rows, gate_cols, preferred_element_type=jnp.float32)
    up_val = jnp.dot(tok_rows, up_cols, preferred_element_type=jnp.float32)
    gate_act = jax.nn.silu(gate_val)
    gate_sig = jax.nn.sigmoid(gate_val)
    hidden = (gate_act * up_val).astype(jnp.bfloat16)
    down_grad = jnp.dot(hidden.T, scaled_rows, preferred_element_type=jnp.float32).astype(jnp.bfloat16)
    hidden_grad = jnp.dot(scaled_rows, down_rows.T, preferred_element_type=jnp.float32)
    act_slope = gate_sig * (1.0 + gate_val * (1.0 - gate_sig))
    gate_delta = (hidden_grad * up_val * act_slope).astype(jnp.bfloat16)
    up_delta = (hidden_grad * gate_act).astype(jnp.bfloat16)
    gate_grad = jnp.dot(tok_rows.T, gate_delta, preferred_element_type=jnp.float32).astype(jnp.bfloat16)
    up_grad = jnp.dot(tok_rows.T, up_delta, preferred_element_type=jnp.float32).astype(jnp.bfloat16)
    split_gate = barrier_float(gate_delta).reshape(-1, SHARDS, FFD)
    split_up = barrier_float(up_delta).reshape(-1, SHARDS, FFD)
    gate_shards = gate_cols.astype(jnp.float32).reshape(D, SHARDS, FFD)
    up_shards = up_cols.astype(jnp.float32).reshape(D, SHARDS, FFD)
    shard_parts = jnp.einsum("rsf,dsf->srd", split_gate, gate_shards) + jnp.einsum("rsf,dsf->srd", split_up, up_shards)
    return shard_total(shard_parts), gate_grad, up_grad, down_grad


def reference(front_tokens, front_routes, front_mixing, back_tokens, back_routes, back_mixing, back_upstream, gate_weight, up_weight, down_weight):
    front_list = []
    token_list = []
    grads_list = []
    for section_index in range(N_PIPE):
        gate_all = gate_weight[section_index].reshape(D, EXPERTS, FFW).transpose(1, 0, 2)
        up_all = up_weight[section_index].reshape(D, EXPERTS, FFW).transpose(1, 0, 2)
        down_all = down_weight[section_index].reshape(EXPERTS, FFW, D)

        routes = front_routes[section_index]
        slot_index = slot_table(routes)
        mixing = front_mixing[section_index].astype(jnp.float32) * weight_unit
        copied_rows = jnp.broadcast_to(front_tokens[section_index][:, None, :], (TOKENS, TOP, D))
        front_rows = scatter_rows(copied_rows, routes, slot_index)
        front_slots = lax.map(forward_expert, (front_rows, gate_all, up_all, down_all))
        picked = front_slots[routes, slot_index].astype(jnp.float32)
        front_list.append(jnp.sum(mixing[:, :, None] * picked, axis=1).astype(jnp.bfloat16))

        routes = back_routes[section_index]
        slot_index = slot_table(routes)
        mixing = back_mixing[section_index].astype(jnp.float32) * weight_unit
        copied_rows = jnp.broadcast_to(back_tokens[section_index][:, None, :], (TOKENS, TOP, D))
        back_rows = scatter_rows(copied_rows, routes, slot_index)
        scaled = (mixing[:, :, None] * back_upstream[section_index].astype(jnp.float32)[:, None, :]).astype(jnp.bfloat16)
        scaled_rows = scatter_rows(scaled, routes, slot_index)
        grad_slots, gate_section, up_section, down_section = lax.map(backward_expert, (back_rows, scaled_rows, gate_all, up_all, down_all))
        picked = grad_slots[routes, slot_index].astype(jnp.float32)
        token_list.append(jnp.sum(picked, axis=1).astype(jnp.bfloat16))
        grads_list.append((gate_section.transpose(1, 0, 2).reshape(D, EXPERTS * FFW), up_section.transpose(1, 0, 2).reshape(D, EXPERTS * FFW), down_section.reshape(EXPERTS * FFW, D)))

    half_rows = D // 2
    gate_out = []
    up_out = []
    down_out = []
    for section_index in range(N_PIPE):
        mirror = N_PIPE - 1 - section_index
        start_row = half_rows if 2 * section_index >= N_PIPE else 0
        gate_sum = (barrier_float(grads_list[section_index][0]) + barrier_float(grads_list[mirror][0])).astype(jnp.bfloat16)
        up_sum = (barrier_float(grads_list[section_index][1]) + barrier_float(grads_list[mirror][1])).astype(jnp.bfloat16)
        down_sum = (barrier_float(grads_list[section_index][2]) + barrier_float(grads_list[mirror][2])).astype(jnp.bfloat16)
        gate_out.append(gate_sum[start_row:start_row + half_rows])
        up_out.append(up_sum[start_row:start_row + half_rows])
        down_out.append(down_sum[:, start_row:start_row + half_rows])
    return (jnp.stack(front_list), jnp.stack(token_list), jnp.stack(gate_out), jnp.stack(up_out), jnp.stack(down_out))
```

```python
import functools

import jax
import jax.numpy as jnp
from jax import lax
from jax.experimental import pallas as pl
from jax.experimental.pallas import tpu as pltpu
from jax.sharding import PartitionSpec as P

SHARDS = 8
LANES = 128
TOP = 2

weight_unit = 0.0625


def token_weights(routes, mixing):
    hits = routes[:, :, None] == jnp.arange(LANES, dtype=jnp.int32)[None, None, :]
    weights = mixing.astype(jnp.float32) * weight_unit
    return jnp.sum(jnp.where(hits, weights[:, :, None], 0.0), axis=1).astype(jnp.bfloat16)


def rows_dot(rows, matrix, dim):
    return lax.dot_general(
        rows, matrix, (((2,), (dim,)), ((), ())), preferred_element_type=jnp.float32
    )


def grad_dot(rows, deltas):
    return lax.dot_general(
        rows, deltas, (((0, 1), (0, 1)), ((), ())), preferred_element_type=jnp.float32
    ).astype(jnp.bfloat16)


def local_collectives(
    front_tokens,
    front_routes,
    front_mixing,
    back_tokens,
    back_routes,
    back_mixing,
    back_upstream,
    gate_weight,
    up_weight,
    down_weight,
):
    tokens = front_tokens.shape[1]
    features = front_tokens.shape[2]
    gate_cols = gate_weight[0]
    up_cols = up_weight[0]
    down_rows = down_weight[0]
    expert = lax.axis_index("expert") // SHARDS
    picked = (jnp.arange(LANES, dtype=jnp.int32) == expert).astype(jnp.float32)

    front_table = token_weights(front_routes[0], front_mixing[0])
    back_table = token_weights(back_routes[0], back_mixing[0])
    back_load = jnp.concatenate(
        [
            jnp.concatenate([back_tokens[0], jnp.zeros_like(back_table)], axis=1),
            jnp.concatenate([back_upstream[0], back_table], axis=1),
        ],
        axis=0,
    )
    front_load = jnp.concatenate([front_tokens[0], front_table], axis=1)
    back_all = lax.all_gather(back_load, "expert", axis=0)
    front_all = lax.all_gather(front_load, "expert", axis=0)

    def own_weight(table):
        return jnp.sum(table.astype(jnp.float32) * picked, axis=2, keepdims=True)

    back_rows = back_all[:, :tokens, :features]
    upstream = back_all[:, tokens:, :features]
    back_scale = own_weight(back_all[:, tokens:, features:])
    scaled_rows = (upstream.astype(jnp.float32) * back_scale).astype(jnp.bfloat16)
    back_gate = rows_dot(back_rows, gate_cols, 0)
    back_up = rows_dot(back_rows, up_cols, 0)
    hidden_grad = rows_dot(scaled_rows, down_rows, 1)
    gate_sig = jax.nn.sigmoid(back_gate)
    gate_act = back_gate * gate_sig
    back_hidden = (gate_act * back_up).astype(jnp.bfloat16)
    act_slope = gate_sig * (1.0 + back_gate * (1.0 - gate_sig))
    gate_delta = (hidden_grad * back_up * act_slope).astype(jnp.bfloat16)
    up_delta = (hidden_grad * gate_act).astype(jnp.bfloat16)
    sections = jnp.stack(
        [
            grad_dot(back_rows, gate_delta),
            grad_dot(back_rows, up_delta),
            grad_dot(scaled_rows, back_hidden),
        ]
    )
    pipe_count = lax.axis_size("pipe")
    half = features // 2
    upper = lax.axis_index("pipe") * 2 >= pipe_count
    own_start = jnp.where(upper, half, 0)
    own_half = lax.dynamic_slice_in_dim(sections, own_start, half, axis=1)
    leaving = lax.dynamic_slice_in_dim(sections, half - own_start, half, axis=1)
    arrived = lax.ppermute(leaving, "pipe", [(p, pipe_count - 1 - p) for p in range(pipe_count)])

    back_parts = (rows_dot(gate_delta, gate_cols, 1) + rows_dot(up_delta, up_cols, 1)).astype(
        jnp.bfloat16
    )
    front_rows = front_all[:, :, :features]
    front_scale = own_weight(front_all[:, :, features:])
    front_gate = rows_dot(front_rows, gate_cols, 0)
    front_up = rows_dot(front_rows, up_cols, 0)
    front_hidden = (jax.nn.silu(front_gate) * front_up).astype(jnp.bfloat16)
    front_parts = (rows_dot(front_hidden, down_rows, 0) * front_scale).astype(jnp.bfloat16)
    totals = lax.psum_scatter(
        jnp.concatenate([front_parts, back_parts], axis=1), "expert", scatter_dimension=0
    )
    summed = (own_half.astype(jnp.float32) + arrived.astype(jnp.float32)).astype(jnp.bfloat16)
    return (
        totals[:tokens][None],
        totals[tokens:][None],
        summed[0][None],
        summed[1][None],
        summed[2].T[None],
    )


MESH = pl.DeviceIdType.MESH
TOK = 12
EXPERTS = 2
ZS, YS, CS = 4, 2, 2
CHIPS = ZS * YS
BLOCKS = CHIPS * CS
HID = 128
PAIR = 2 * TOK
FOLD = 2 * PAIR
DEPTH = CHIPS * FOLD
SLOTS = CHIPS * PAIR
GROUPS = ((0, 2), (2, 2), (4, 3))
VMEM_LIMIT = 48 * 1024 * 1024


def nn(a, b):
    return jnp.dot(a, b, preferred_element_type=jnp.float32)


def nt(a, b):
    return lax.dot_general(a, b, (((1,), (1,)), ((), ())), preferred_element_type=jnp.float32)


def tn(a, b):
    return lax.dot_general(a, b, (((0,), (0,)), ((), ())), preferred_element_type=jnp.float32)


def kernel(
    features,
    back_hbm, up_hbm, front_hbm, broutes_hbm, bmix_hbm, froutes_hbm, fmix_hbm, gate_hbm, up_w_hbm, down_hbm,
    front_out, back_out, gate_out, up_out, dn_out,
    stage, mix, gate_w, up_w, down_w, wide, ex_send, ex_recv, xs, ms, tab, tabs, sc, dc, dsend, dm, de,
    r32, drs, ers, pb, rc, ry, zsb, rz, tot,
    local_sems, ex_sems, zs, zr, ys, yr, cs, cr, xsem, xrem, mcs, mcr, ts, tr, dms, rs, rr,
):
    f32, bf = jnp.float32, jnp.bfloat16
    me = lax.axis_index("expert")
    pipe = lax.axis_index("pipe")
    c = me % CS
    y = (me // CS) % YS
    z = me // (CS * YS)
    k = me // SHARDS
    quarter = features // 4
    half = features // 2

    def dev(zz, yy, cc):
        return {"expert": (zz * YS + yy) * CS + cc}

    zpeer = [None] + [(z + d) % ZS for d in range(1, ZS)]
    zfrom = [None] + [(z + ZS - d) % ZS for d in range(1, ZS)]
    core_dev = dev(z, y, 1 - c)
    y_dev = dev(z, 1 - y, c)
    z_dev = [None] + [dev(zpeer[d], y, c) for d in range(1, ZS)]
    mirror = {"pipe": 1 - pipe}
    low = z < 2
    inner = jnp.where(low, z, 3 - z)

    def real(s):
        return jnp.where(low, s, 3 - s)

    sources = [z, real(1 - inner), real(2), real(3)]
    z_in = dev(real(1 + inner), y, c)
    z_out = dev(real(0), y, c)

    loads = [
        pltpu.make_async_copy(src, dst, local_sems.at[i])
        for i, (src, dst) in enumerate(
            [
                (back_hbm, stage.at[0]), (up_hbm, stage.at[1]), (front_hbm, stage.at[2]),
                (froutes_hbm, mix.at[0]), (fmix_hbm, mix.at[1]), (broutes_hbm, mix.at[2]), (bmix_hbm, mix.at[3]),
                (gate_hbm, gate_w), (up_w_hbm, up_w), (down_hbm, down_w),
            ]
        )
    ]
    for load in loads:
        load.start()

    barrier = pltpu.get_barrier_semaphore()
    for target in [core_dev, y_dev, z_dev[1], z_dev[2], z_dev[3], mirror]:
        pl.semaphore_signal(barrier, inc=1, device_id=target, device_id_type=MESH)

    lanes = lax.broadcasted_iota(jnp.int32, (TOK, LANES), 1)
    square = (TOK, TOK)
    diagonal = lax.broadcasted_iota(jnp.int32, square, 0) == lax.broadcasted_iota(jnp.int32, square, 1)

    def upright(row):
        wide_row = jnp.broadcast_to(row.astype(f32), square)
        return jnp.sum(jnp.where(diagonal, wide_row, 0.0), axis=1, keepdims=True)

    def table(routes, mixing, base):
        out = jnp.zeros((TOK, LANES), f32)
        for j in range(TOP):
            weight = upright(mixing[j : j + 1]) * weight_unit
            out = out + jnp.where(upright(routes[j : j + 1]).astype(jnp.int32) + base == lanes, weight, 0.0)
        return out

    chip = y * ZS + z
    own_tab = c * CHIPS + chip

    for load in loads[:7]:
        load.wait()
    for a in range(3):
        rows = stage[a].astype(f32)
        for h in range(2):
            for q in range(2):
                at = (2 * h + q) * quarter
                piece = rows[:, at : at + quarter]
                for cc in range(2):
                    top = q * PAIR + cc * TOK
                    wide[a, h, top : top + TOK, :] = jnp.where(c == cc, piece, 0.0)
    for a in range(3):
        ex_send[a] = wide[a, 1 - c].astype(bf)
    tab[...] = jnp.zeros_like(tab)
    tab[0:TOK, :] = table(mix[2], mix[3], 0) + table(mix[0], mix[1], EXPERTS)
    tabs[own_tab] = tab[...].astype(bf)
    pl.semaphore_wait(barrier, 6)

    def remote(src, dst, ssem, rsem, target):
        return pltpu.make_async_remote_copy(
            src_ref=src, dst_ref=dst, send_sem=ssem, recv_sem=rsem,
            device_id=target, device_id_type=MESH,
        )

    def exchange(i):
        part = pl.ds(0, 2) if i == 0 else pl.ds(2, 1)
        return remote(ex_send.at[part], ex_recv.at[part], ex_sems.at[0, i], ex_sems.at[1, i], core_dev)

    exchange(0).start()
    exchange(1).start()

    def tab_z(d):
        return remote(tabs.at[own_tab], tabs.at[own_tab], ts.at[d], tr.at[d], z_dev[d])

    def tab_z_arrival(d):
        at = c * CHIPS + y * ZS + zfrom[d]
        return remote(tabs.at[at], tabs.at[at], ts.at[d], tr.at[d], z_dev[d])

    def tab_y(yy):
        part = tabs.at[pl.ds(c * CHIPS + yy * ZS, ZS)]
        return remote(part, part, ts.at[0], tr.at[0], y_dev)

    def tab_c(cc):
        part = tabs.at[pl.ds(cc * CHIPS, CHIPS)]
        return remote(part, part, ts.at[4], tr.at[4], core_dev)

    for d in (1, 2, 3):
        tab_z(d).start()

    def rows_of(zz, yy):
        return pl.ds(pl.multiple_of((yy * ZS + zz) * FOLD, 16), FOLD)

    def block(a, h, zz, yy):
        return xs.at[a, h, rows_of(zz, yy)]

    def z_copy(a, slot):
        if slot == 0:
            return remote(block(a, c, z, y), block(a, c, z, y), zs.at[a, 0], zr.at[a, inner], z_in)
        if slot == 1:
            return remote(block(a, c, z, y), block(a, c, z, y), zs.at[a, 1], zr.at[a, 0], z_out)
        i = slot - 1
        at = block(a, c, sources[i], y)
        target, arrival = (z_in, 2) if i == 1 else (z_out, i - 1)
        return remote(at, at, zs.at[a, slot], zr.at[a, arrival], target)

    def z_arrival(a, i):
        at = block(a, c, sources[i], y)
        return remote(at, at, zs.at[a, 0], zr.at[a, i - 1], z_in)

    def y_copy(a, i, yy):
        at = block(a, c, sources[i], yy)
        return remote(at, at, ys.at[a, i], yr.at[a, i], y_dev)

    def c_copy(a, i, far, cc):
        at = block(a, cc, sources[i], 1 - y if far else y)
        return remote(at, at, cs.at[a, 4 * far + i], cr.at[a, 4 * far + i], core_dev)

    def x_copy(i, far):
        rows = rows_of(sources[i], 1 - y if far else y)
        at = 4 * far + i
        return remote(xs.at[c, 1 - pipe, rows], ms.at[c, rows], xsem.at[at], xrem.at[at], mirror)

    def m_copy(far, cc):
        yy = 1 - y if far else y
        rows = pl.ds(pl.multiple_of(yy * ZS * FOLD, 16), ZS * FOLD)
        return remote(ms.at[cc, rows], ms.at[cc, rows], mcs.at[far], mcr.at[far], core_dev)

    def own(a):
        xs[a, c, rows_of(z, y), :] = (wide[a, c] + ex_recv[a].astype(f32)).astype(bf)

    def z_begin(a):
        z_copy(a, 0).start()

        @pl.when(inner == 1)
        def _():
            z_copy(a, 1).start()

    def z_arrive(a, i):
        z_arrival(a, i).wait_recv()

        @pl.when(inner == 1)
        def _():
            z_copy(a, i + 1).start()

    def y_go(a, i):
        y_copy(a, i, y).start()

    def c_go(a, i):
        c_copy(a, i, 0, c).start()

    def y_arrive(a, i):
        y_copy(a, i, 1 - y).wait_recv()
        c_copy(a, i, 1, c).start()

    def mirror_go(i, far):
        for a in (0, 1):
            c_copy(a, i, far, 1 - c).wait_recv()
        x_copy(i, far).start()

    exchange(0).wait_recv()
    for a in (0, 1):
        own(a)
        z_begin(a)
        y_go(a, 0)
        c_go(a, 0)
    exchange(1).wait_recv()
    own(2)
    for a in (0, 1):
        z_arrive(a, 1)
        y_go(a, 1)
        c_go(a, 1)
    z_begin(2)
    c_go(2, 0)
    mirror_go(0, 0)
    for d in (1, 2, 3):
        tab_z_arrival(d).wait_recv()
    tab_y(y).start()
    for a in (0, 1):
        y_arrive(a, 0)
    mirror_go(1, 0)
    for a in (0, 1):
        z_arrive(a, 2)
        y_go(a, 2)
        c_go(a, 2)
    mirror_go(0, 1)
    z_arrive(2, 1)
    c_go(2, 1)
    tab_y(1 - y).wait_recv()
    tab_c(c).start()
    for a in (0, 1):
        y_arrive(a, 1)
    mirror_go(2, 0)
    for a in (0, 1):
        z_arrive(a, 3)
        y_go(a, 3)
        c_go(a, 3)
    y_go(2, 0)
    y_go(2, 1)
    mirror_go(1, 1)
    for a in (0, 1):
        y_arrive(a, 2)
    mirror_go(3, 0)
    z_arrive(2, 2)
    y_go(2, 2)
    c_go(2, 2)
    z_arrive(2, 3)
    y_go(2, 3)
    c_go(2, 3)
    mirror_go(2, 1)
    tab_c(1 - c).wait_recv()
    for b in range(CHIPS):
        for cc in range(CS):
            at = b * PAIR + cc * TOK
            tab[...] = tabs[cc * CHIPS + b].astype(f32)
            sc[at : at + TOK, :] = tab[0:TOK, :]
    for load in loads[7:]:
        load.wait()
    for a in (0, 1):
        y_arrive(a, 3)
    mirror_go(3, 1)

    slot_lanes = lax.broadcasted_iota(jnp.int32, (SLOTS, LANES), 1)

    def scale_of(base):
        return jnp.sum(jnp.where(slot_lanes == k + base, sc[...], 0.0), axis=1, keepdims=True)

    def hidden(a):
        total = None
        for h in range(2):
            parts = []
            for q in range(2):
                at = (2 * h + q) * quarter
                parts += [gate_w[at : at + quarter, :], up_w[at : at + quarter, :]]
            term = nn(xs[a, h], jnp.concatenate(parts, axis=1))
            total = term if total is None else total + term
        total = total.reshape(CHIPS, FOLD, 4 * HID)
        both = total[:, 0:PAIR, 0 : 2 * HID] + total[:, PAIR:, 2 * HID :]
        both = both.reshape(SLOTS, 2 * HID)
        return both[:, 0:HID], both[:, HID:]

    gate, up = hidden(0)
    total = None
    for h in range(2):
        at = 2 * h * quarter
        pair = jnp.concatenate(
            [down_w[:, at : at + quarter], down_w[:, at + quarter : at + 2 * quarter]], axis=0
        )
        term = nt(xs[1, h], pair)
        total = term if total is None else total + term
    total = total.reshape(CHIPS, FOLD, 2 * HID)
    scale = scale_of(0)
    grad = (total[:, 0:PAIR, 0:HID] + total[:, PAIR:, HID:]).reshape(SLOTS, HID) * scale
    sig = 1.0 / (1.0 + jnp.exp(-gate))
    act = gate * sig
    dc[:, 0:HID] = grad * up * (sig * (1.0 + gate * (1.0 - sig)))
    dc[:, HID : 2 * HID] = grad * act
    dc[:, 2 * HID :] = act * up * scale
    dsend[...] = dc[...].astype(bf)
    deltas = remote(dsend, dm, dms.at[0], dms.at[1], mirror)
    deltas.start()
    y_arrive(2, 0)

    def by_device(width):
        for b in range(CHIPS):
            for cc in range(CS):
                at = b * PAIR + cc * TOK
                to = cc * CHIPS * 16 + b * 16
                r32[to : to + TOK, 0:width] = dc[at : at + TOK, 0:width]
                r32[to + TOK : to + 16, 0:width] = dc[at + 8 : at + TOK, 0:width]
        return r32[:, 0:width].astype(bf)

    drs[...] = by_device(2 * HID)

    def core_sum(a, g):
        j, n = GROUPS[g]
        part = pl.ds(j, n)
        return remote(pb.at[a, 1 - c, part], rc.at[a, part], rs.at[a, g, 0], rr.at[a, g, 0], core_dev)

    def y_sum(a, g):
        j, n = GROUPS[g]
        part = pl.ds(j, n)
        rows = pl.ds(pl.multiple_of((1 - y) * ZS * FOLD, 16), ZS * FOLD)
        return remote(pb.at[a, c, part, rows], ry.at[a, part], rs.at[a, g, 4], rr.at[a, g, 4], y_dev)

    def z_sum(a, g, d):
        j, n = GROUPS[g]
        part = pl.ds(j, n)
        rows = pl.ds(pl.multiple_of(zpeer[d] * FOLD, 16), FOLD)
        return remote(zsb.at[a, part, rows], rz.at[a, d - 1, part], rs.at[a, g, d], rr.at[a, g, d], z_dev[d])

    early = lax.broadcasted_iota(jnp.int32, (1, 1, 8, 1), 2) < 4

    def part(a, g):
        j, n = GROUPS[g]
        wide_of = n * LANES
        outs = []
        for q in range(4):
            at = q * quarter + j * LANES
            if a == 0:
                both = jnp.concatenate([gate_w[at : at + wide_of, :], up_w[at : at + wide_of, :]], axis=1)
                out = nt(drs[...], both)
            else:
                out = nn(ers[...], down_w[:, at : at + wide_of])
            outs.append(out.reshape(CS, CHIPS, 16, wide_of))
        tops = [out[:, :, 0:8] for out in outs]
        ends = [jnp.where(early, outs[2 * i][:, :, 8:16], outs[2 * i + 1][:, :, 8:16]) for i in range(2)]
        folded = jnp.concatenate(tops + ends, axis=2).reshape(CS, DEPTH, wide_of).astype(bf)
        for i in range(n):
            pb[a, :, j + i] = folded[:, :, i * LANES : (i + 1) * LANES]
        core_sum(a, g).start()

    def over_cores(a, g):
        j, n = GROUPS[g]
        part = pl.ds(j, n)
        core_sum(a, g).wait_recv()
        for yy in (1 - y, y):
            rows = pl.ds(pl.multiple_of(yy * ZS * FOLD, 16), ZS * FOLD)
            pb[a, c, part, rows, :] = (
                pb[a, c, part, rows, :].astype(f32) + rc[a, part, rows, :].astype(f32)
            ).astype(bf)
            if yy is not y:
                y_sum(a, g).start()

    def over_y(a, g):
        j, n = GROUPS[g]
        part = pl.ds(j, n)
        y_sum(a, g).wait_recv()
        rows = pl.ds(pl.multiple_of(y * ZS * FOLD, 16), ZS * FOLD)
        zsb[a, part] = (pb[a, c, part, rows, :].astype(f32) + ry[a, part].astype(f32)).astype(bf)
        for d in (1, 2, 3):
            z_sum(a, g, d).start()

    def over_z(a, g, out):
        j, n = GROUPS[g]
        part = pl.ds(j, n)
        rows = pl.ds(pl.multiple_of(z * FOLD, 16), FOLD)
        total = zsb[a, part, rows, :].astype(f32)
        for d in (1, 2, 3):
            z_sum(a, g, d).wait_recv()
            total = total + rz[a, d - 1, part].astype(f32)
        tot[part] = total
        for i in range(n):
            for q in range(4):
                piece = jnp.concatenate(
                    [tot[j + i, 8 * q : 8 * q + 8], tot[j + i, 32 + 4 * q : 36 + 4 * q]], axis=0
                )
                at = q * quarter + (j + i) * LANES
                out[:, at : at + LANES] = piece.astype(bf)

    part(0, 0)
    y_arrive(2, 1)
    part(0, 1)
    over_cores(0, 0)
    y_arrive(2, 2)
    part(0, 2)
    over_cores(0, 1)
    y_arrive(2, 3)
    over_cores(0, 2)
    for far in (0, 1):
        for i in range(4):
            x_copy(i, far).wait_recv()
        m_copy(far, c).start()
    for far in (0, 1):
        for i in range(4):
            c_copy(2, i, far, 1 - c).wait_recv()
    gate, up = hidden(2)
    dc[:, 0:HID] = gate / (1.0 + jnp.exp(-gate)) * up * scale_of(EXPERTS)
    ers[...] = by_device(HID)
    part(1, 0)
    over_y(0, 0)
    part(1, 1)
    over_cores(1, 0)
    over_y(0, 1)
    part(1, 2)
    over_cores(1, 1)
    over_y(0, 2)
    over_cores(1, 2)
    over_z(0, 0, back_out)
    deltas.wait_recv()

    def spread(rows):
        rows = rows.reshape(CHIPS, PAIR, 3 * HID)
        pair, last = rows[:, :, 0 : 2 * HID], rows[:, :, 2 * HID :]
        empty, short = jnp.zeros_like(pair), jnp.zeros_like(last)
        first = jnp.concatenate([pair, empty, last, short], axis=2)
        second = jnp.concatenate([empty, pair, short, last], axis=2)
        return jnp.concatenate([first, second], axis=1).reshape(DEPTH, 6 * HID).astype(bf)

    de[0:DEPTH, :] = spread(dsend[...].astype(f32))
    de[DEPTH:, :] = spread(dm[...].astype(f32))
    over_y(1, 0)
    for far in (0, 1):
        m_copy(far, 1 - c).wait_recv()

    def grads(g):
        j, n = GROUPS[g]
        cols = slice(j * LANES, (j + n) * LANES)
        size = n * LANES
        both = tn(jnp.concatenate([xs[0, pipe, :, cols], ms[0, :, cols]], axis=0), de[:, 0 : 4 * HID]).astype(bf)
        last = tn(de[:, 4 * HID :], jnp.concatenate([xs[1, pipe, :, cols], ms[1, :, cols]], axis=0)).astype(bf)
        for q in range(2):
            at = q * quarter + j * LANES
            gate_out[at : at + size, :] = both[:, 2 * q * HID : (2 * q + 1) * HID]
            up_out[at : at + size, :] = both[:, (2 * q + 1) * HID : (2 * q + 2) * HID]
            dn_out[:, at : at + size] = last[q * HID : (q + 1) * HID]

    grads(0)
    over_z(0, 1, back_out)
    over_y(1, 1)
    grads(1)
    over_z(0, 2, back_out)
    over_y(1, 2)
    grads(2)
    for g in range(len(GROUPS)):
        over_z(1, g, front_out)

    for i in (0, 1):
        exchange(i).wait_send()
    for a in range(3):
        z_copy(a, 0).wait_send()

        @pl.when(inner == 1)
        def _():
            for slot in range(1, 5):
                z_copy(a, slot).wait_send()

        for i in range(4):
            y_copy(a, i, y).wait_send()
            for far in (0, 1):
                c_copy(a, i, far, c).wait_send()
    for far in (0, 1):
        for i in range(4):
            x_copy(i, far).wait_send()
        m_copy(far, c).wait_send()
    for d in (1, 2, 3):
        tab_z(d).wait_send()
    tab_y(y).wait_send()
    tab_c(c).wait_send()
    deltas.wait_send()
    for a in range(2):
        for g in range(len(GROUPS)):
            core_sum(a, g).wait_send()
            y_sum(a, g).wait_send()
            for d in (1, 2, 3):
                z_sum(a, g, d).wait_send()


def place(*refs):
    count = len(refs) // 2
    for i in range(count):
        refs[count + i][...] = refs[i][...]


def local_kernel(
    front_tokens, front_routes, front_mixing, back_tokens, back_routes, back_mixing,
    back_upstream, gate_weight, up_weight, down_weight,
):
    features = front_tokens.shape[2]
    half = features // 2
    quarter = features // 4
    tiles = quarter // LANES
    bf, f32 = jnp.bfloat16, jnp.float32
    vm = pltpu.VMEM
    dma = pltpu.SemaphoreType.DMA
    results = pl.pallas_call(
        functools.partial(kernel, features),
        out_shape=[
            jax.ShapeDtypeStruct((TOK, features), bf),
            jax.ShapeDtypeStruct((TOK, features), bf),
            jax.ShapeDtypeStruct((half, HID), bf),
            jax.ShapeDtypeStruct((half, HID), bf),
            jax.ShapeDtypeStruct((HID, half), bf),
        ],
        in_specs=[pl.BlockSpec(memory_space=pltpu.MemorySpace.HBM)] * 10,
        out_specs=[pl.BlockSpec(memory_space=vm)] * 5,
        scratch_shapes=[
            vm((3, TOK, features), bf),
            vm((4, TOP, TOK), jnp.int32),
            vm((features, HID), bf),
            vm((features, HID), bf),
            vm((HID, features), bf),
            vm((3, 2, FOLD, quarter), f32),
            vm((3, FOLD, quarter), bf),
            vm((3, FOLD, quarter), bf),
            vm((3, 2, DEPTH, quarter), bf),
            vm((2, DEPTH, quarter), bf),
            vm((16, LANES), f32),
            vm((BLOCKS, 16, LANES), bf),
            vm((SLOTS, LANES), f32),
            vm((SLOTS, 3 * HID), f32),
            vm((SLOTS, 3 * HID), bf),
            vm((SLOTS, 3 * HID), bf),
            vm((2 * DEPTH, 6 * HID), bf),
            vm((BLOCKS * 16, 2 * HID), f32),
            vm((BLOCKS * 16, 2 * HID), bf),
            vm((BLOCKS * 16, HID), bf),
            vm((2, CS, tiles, DEPTH, LANES), bf),
            vm((2, tiles, DEPTH, LANES), bf),
            vm((2, tiles, ZS * FOLD, LANES), bf),
            vm((2, tiles, ZS * FOLD, LANES), bf),
            vm((2, ZS - 1, tiles, FOLD, LANES), bf),
            vm((tiles, FOLD, LANES), f32),
            dma((10,)), dma((2, 2)),
            dma((3, 5)), dma((3, 3)), dma((3, 4)), dma((3, 4)), dma((3, 8)), dma((3, 8)),
            dma((8,)), dma((8,)), dma((2,)), dma((2,)), dma((5,)), dma((5,)), dma((2,)),
            dma((2, len(GROUPS), 5)), dma((2, len(GROUPS), 5)),
        ],
        compiler_params=pltpu.CompilerParams(
            collective_id=0, has_side_effects=True, vmem_limit_bytes=VMEM_LIMIT
        ),
    )(
        back_tokens[0], back_upstream[0], front_tokens[0], back_routes[0].T, back_mixing[0].T,
        front_routes[0].T, front_mixing[0].T, gate_weight[0], up_weight[0], down_weight[0],
    )
    front, back, gate, up, down = pl.pallas_call(
        place,
        out_shape=[jax.ShapeDtypeStruct(item.shape, item.dtype) for item in results],
        in_specs=[pl.BlockSpec(memory_space=vm)] * 5,
        out_specs=[pl.BlockSpec(memory_space=vm)] * 5,
        compiler_params=pltpu.CompilerParams(vmem_limit_bytes=VMEM_LIMIT),
    )(*results)
    return front[None], back[None], gate[None], up[None], down[None]


def solution(mesh):
    fits = mesh.shape["pipe"] == 2 and mesh.shape["expert"] == BLOCKS
    local = local_kernel if fits else local_collectives
    rows = P("pipe", "expert", None)
    columns = P("pipe", None, "expert")
    return jax.shard_map(
        local,
        mesh=mesh,
        in_specs=(rows,) * 7 + (columns, columns, rows),
        out_specs=(rows, rows, columns, columns, rows),
        check_vma=False,
    )
```

```python
import functools

import jax
import jax.numpy as jnp
from jax import lax
from jax.experimental import pallas as pl
from jax.experimental.pallas import tpu as pltpu
from jax.sharding import PartitionSpec as P

SHARDS = 8
LANES = 128
TOP = 2

weight_unit = 0.0625


def token_weights(routes, mixing):
    hits = routes[:, :, None] == jnp.arange(LANES, dtype=jnp.int32)[None, None, :]
    weights = mixing.astype(jnp.float32) * weight_unit
    return jnp.sum(jnp.where(hits, weights[:, :, None], 0.0), axis=1).astype(jnp.bfloat16)


def rows_dot(rows, matrix, dim):
    return lax.dot_general(
        rows, matrix, (((2,), (dim,)), ((), ())), preferred_element_type=jnp.float32
    )


def grad_dot(rows, deltas):
    return lax.dot_general(
        rows, deltas, (((0, 1), (0, 1)), ((), ())), preferred_element_type=jnp.float32
    ).astype(jnp.bfloat16)


def local_collectives(
    front_tokens,
    front_routes,
    front_mixing,
    back_tokens,
    back_routes,
    back_mixing,
    back_upstream,
    gate_weight,
    up_weight,
    down_weight,
):
    tokens = front_tokens.shape[1]
    features = front_tokens.shape[2]
    gate_cols = gate_weight[0]
    up_cols = up_weight[0]
    down_rows = down_weight[0]
    expert = lax.axis_index("expert") // SHARDS
    picked = (jnp.arange(LANES, dtype=jnp.int32) == expert).astype(jnp.float32)

    front_table = token_weights(front_routes[0], front_mixing[0])
    back_table = token_weights(back_routes[0], back_mixing[0])
    back_load = jnp.concatenate(
        [
            jnp.concatenate([back_tokens[0], jnp.zeros_like(back_table)], axis=1),
            jnp.concatenate([back_upstream[0], back_table], axis=1),
        ],
        axis=0,
    )
    front_load = jnp.concatenate([front_tokens[0], front_table], axis=1)
    back_all = lax.all_gather(back_load, "expert", axis=0)
    front_all = lax.all_gather(front_load, "expert", axis=0)

    def own_weight(table):
        return jnp.sum(table.astype(jnp.float32) * picked, axis=2, keepdims=True)

    back_rows = back_all[:, :tokens, :features]
    upstream = back_all[:, tokens:, :features]
    back_scale = own_weight(back_all[:, tokens:, features:])
    scaled_rows = (upstream.astype(jnp.float32) * back_scale).astype(jnp.bfloat16)
    back_gate = rows_dot(back_rows, gate_cols, 0)
    back_up = rows_dot(back_rows, up_cols, 0)
    hidden_grad = rows_dot(scaled_rows, down_rows, 1)
    gate_sig = jax.nn.sigmoid(back_gate)
    gate_act = back_gate * gate_sig
    back_hidden = (gate_act * back_up).astype(jnp.bfloat16)
    act_slope = gate_sig * (1.0 + back_gate * (1.0 - gate_sig))
    gate_delta = (hidden_grad * back_up * act_slope).astype(jnp.bfloat16)
    up_delta = (hidden_grad * gate_act).astype(jnp.bfloat16)
    sections = jnp.stack(
        [
            grad_dot(back_rows, gate_delta),
            grad_dot(back_rows, up_delta),
            grad_dot(scaled_rows, back_hidden),
        ]
    )
    pipe_count = lax.axis_size("pipe")
    half = features // 2
    upper = lax.axis_index("pipe") * 2 >= pipe_count
    own_start = jnp.where(upper, half, 0)
    own_half = lax.dynamic_slice_in_dim(sections, own_start, half, axis=1)
    leaving = lax.dynamic_slice_in_dim(sections, half - own_start, half, axis=1)
    arrived = lax.ppermute(leaving, "pipe", [(p, pipe_count - 1 - p) for p in range(pipe_count)])

    back_parts = (rows_dot(gate_delta, gate_cols, 1) + rows_dot(up_delta, up_cols, 1)).astype(
        jnp.bfloat16
    )
    front_rows = front_all[:, :, :features]
    front_scale = own_weight(front_all[:, :, features:])
    front_gate = rows_dot(front_rows, gate_cols, 0)
    front_up = rows_dot(front_rows, up_cols, 0)
    front_hidden = (jax.nn.silu(front_gate) * front_up).astype(jnp.bfloat16)
    front_parts = (rows_dot(front_hidden, down_rows, 0) * front_scale).astype(jnp.bfloat16)
    totals = lax.psum_scatter(
        jnp.concatenate([front_parts, back_parts], axis=1), "expert", scatter_dimension=0
    )
    summed = (own_half.astype(jnp.float32) + arrived.astype(jnp.float32)).astype(jnp.bfloat16)
    return (
        totals[:tokens][None],
        totals[tokens:][None],
        summed[0][None],
        summed[1][None],
        summed[2].T[None],
    )


MESH = pl.DeviceIdType.MESH
TOK = 12
EXPERTS = 2
ZS, YS, CS = 4, 2, 2
CHIPS = ZS * YS
BLOCKS = CHIPS * CS
HID = 128
PAIR = 2 * TOK
FOLD = 2 * PAIR
DEPTH = CHIPS * FOLD
SLOTS = CHIPS * PAIR
GROUPS = ((0, 2), (2, 2), (4, 3))
VMEM_LIMIT = 61 * 1024 * 1024


def nn(a, b):
    return jnp.dot(a, b, preferred_element_type=jnp.float32)


def nt(a, b):
    return lax.dot_general(a, b, (((1,), (1,)), ((), ())), preferred_element_type=jnp.float32)


def tn(a, b):
    return lax.dot_general(a, b, (((0,), (0,)), ((), ())), preferred_element_type=jnp.float32)


def kernel(
    features,
    back_hbm, up_hbm, front_hbm, broutes_hbm, bmix_hbm, froutes_hbm, fmix_hbm, gate_hbm, up_w_hbm, down_hbm,
    front_out, back_out, gate_out, up_out, dn_out,
    stage, mix, gate_w, up_w, down_w, wide, ex_send, ex_recv, xs, ms, tab, tabs, sc, dc, dsend, dm, de,
    r32, drs, ers, pb, rc, ry, zsb, rz, tot,
    local_sems, ex_sems, zs, zr, ys, yr, cs, cr, xsem, xrem, mcs, mcr, ts, tr, dms, rs, rr,
):
    f32, bf = jnp.float32, jnp.bfloat16
    me = lax.axis_index("expert")
    pipe = lax.axis_index("pipe")
    c = me % CS
    y = (me // CS) % YS
    z = me // (CS * YS)
    k = me // SHARDS
    quarter = features // 4
    half = features // 2

    def dev(zz, yy, cc):
        return {"expert": (zz * YS + yy) * CS + cc}

    zpeer = [None] + [(z + d) % ZS for d in range(1, ZS)]
    zfrom = [None] + [(z + ZS - d) % ZS for d in range(1, ZS)]
    core_dev = dev(z, y, 1 - c)
    y_dev = dev(z, 1 - y, c)
    z_dev = [None] + [dev(zpeer[d], y, c) for d in range(1, ZS)]
    mirror = {"pipe": 1 - pipe}
    low = z < 2
    inner = jnp.where(low, z, 3 - z)

    def real(s):
        return jnp.where(low, s, 3 - s)

    sources = [z, real(1 - inner), real(2), real(3)]
    z_in = dev(real(1 + inner), y, c)
    z_out = dev(real(0), y, c)

    loads = [
        pltpu.make_async_copy(src, dst, local_sems.at[i])
        for i, (src, dst) in enumerate(
            [
                (back_hbm, stage.at[0]), (up_hbm, stage.at[1]), (front_hbm, stage.at[2]),
                (froutes_hbm, mix.at[0]), (fmix_hbm, mix.at[1]), (broutes_hbm, mix.at[2]), (bmix_hbm, mix.at[3]),
                (gate_hbm, gate_w), (up_w_hbm, up_w), (down_hbm, down_w),
            ]
        )
    ]
    for load in loads:
        load.start()

    barrier = pltpu.get_barrier_semaphore()
    for target in [core_dev, y_dev, z_dev[1], z_dev[2], z_dev[3], mirror]:
        pl.semaphore_signal(barrier, inc=1, device_id=target, device_id_type=MESH)

    lanes = lax.broadcasted_iota(jnp.int32, (TOK, LANES), 1)
    square = (TOK, TOK)
    diagonal = lax.broadcasted_iota(jnp.int32, square, 0) == lax.broadcasted_iota(jnp.int32, square, 1)

    def upright(row):
        wide_row = jnp.broadcast_to(row.astype(f32), square)
        return jnp.sum(jnp.where(diagonal, wide_row, 0.0), axis=1, keepdims=True)

    def table(routes, mixing, base):
        out = jnp.zeros((TOK, LANES), f32)
        for j in range(TOP):
            weight = upright(mixing[j : j + 1]) * weight_unit
            out = out + jnp.where(upright(routes[j : j + 1]).astype(jnp.int32) + base == lanes, weight, 0.0)
        return out

    chip = y * ZS + z
    own_tab = c * CHIPS + chip

    for load in loads[:7]:
        load.wait()
    for a in range(3):
        rows = stage[a].astype(f32)
        for h in range(2):
            for q in range(2):
                at = (2 * h + q) * quarter
                piece = rows[:, at : at + quarter]
                for cc in range(2):
                    top = q * PAIR + cc * TOK
                    wide[a, h, top : top + TOK, :] = jnp.where(c == cc, piece, 0.0)
    for a in range(3):
        ex_send[a] = wide[a, 1 - c].astype(bf)
    tab[...] = jnp.zeros_like(tab)
    tab[0:TOK, :] = table(mix[2], mix[3], 0) + table(mix[0], mix[1], EXPERTS)
    tabs[own_tab] = tab[...].astype(bf)
    pl.semaphore_wait(barrier, 6)

    def remote(src, dst, ssem, rsem, target):
        return pltpu.make_async_remote_copy(
            src_ref=src, dst_ref=dst, send_sem=ssem, recv_sem=rsem,
            device_id=target, device_id_type=MESH,
        )

    def exchange(i):
        part = pl.ds(0, 2) if i == 0 else pl.ds(2, 1)
        return remote(ex_send.at[part], ex_recv.at[part], ex_sems.at[0, i], ex_sems.at[1, i], core_dev)

    exchange(0).start()
    exchange(1).start()

    def tab_z(d):
        return remote(tabs.at[own_tab], tabs.at[own_tab], ts.at[d], tr.at[d], z_dev[d])

    def tab_z_arrival(d):
        at = c * CHIPS + y * ZS + zfrom[d]
        return remote(tabs.at[at], tabs.at[at], ts.at[d], tr.at[d], z_dev[d])

    def tab_y(yy):
        part = tabs.at[pl.ds(c * CHIPS + yy * ZS, ZS)]
        return remote(part, part, ts.at[0], tr.at[0], y_dev)

    def tab_c(cc):
        part = tabs.at[pl.ds(cc * CHIPS, CHIPS)]
        return remote(part, part, ts.at[4], tr.at[4], core_dev)

    for d in (1, 2, 3):
        tab_z(d).start()

    def rows_of(zz, yy):
        return pl.ds(pl.multiple_of((yy * ZS + zz) * FOLD, 16), FOLD)

    def block(a, h, zz, yy):
        return xs.at[a, h, rows_of(zz, yy)]

    def z_copy(a, slot, far=0):
        yy = 1 - y if far else y
        own_at = block(a, c, z, yy)
        if slot == 0:
            return remote(own_at, own_at, zs.at[a + far, 0], zr.at[a + far, inner], z_in)
        if slot == 1:
            return remote(own_at, own_at, zs.at[a + far, 1], zr.at[a + far, 0], z_out)
        i = slot - 1
        at = block(a, c, sources[i], yy)
        target, arrival = (z_in, 2) if i == 1 else (z_out, i - 1)
        return remote(at, at, zs.at[a + far, slot], zr.at[a + far, arrival], target)

    def z_arrival(a, i, far=0):
        at = block(a, c, sources[i], 1 - y if far else y)
        return remote(at, at, zs.at[a + far, 0], zr.at[a + far, i - 1], z_in)

    def y_copy(a, i, yy):
        at = block(a, c, sources[i], yy)
        return remote(at, at, ys.at[a, i], yr.at[a, i], y_dev)

    def c_copy(a, i, far, cc):
        at = block(a, cc, sources[i], 1 - y if far else y)
        return remote(at, at, cs.at[a, 4 * far + i], cr.at[a, 4 * far + i], core_dev)

    def x_copy(i, far):
        rows = rows_of(sources[i], 1 - y if far else y)
        at = 4 * far + i
        return remote(xs.at[c, 1 - pipe, rows], ms.at[c, rows], xsem.at[at], xrem.at[at], mirror)

    def m_copy(far, cc):
        yy = 1 - y if far else y
        rows = pl.ds(pl.multiple_of(yy * ZS * FOLD, 16), ZS * FOLD)
        return remote(ms.at[cc, rows], ms.at[cc, rows], mcs.at[far], mcr.at[far], core_dev)

    def own(a):
        xs[a, c, rows_of(z, y), :] = (wide[a, c] + ex_recv[a].astype(f32)).astype(bf)

    def z_begin(a, far=0):
        z_copy(a, 0, far).start()

        @pl.when(inner == 1)
        def _():
            z_copy(a, 1, far).start()

    def z_arrive(a, i, far=0):
        z_arrival(a, i, far).wait_recv()

        @pl.when(inner == 1)
        def _():
            z_copy(a, i + 1, far).start()

    def y_go(a, i):
        y_copy(a, i, y).start()

    def c_go(a, i, far=0):
        c_copy(a, i, far, c).start()

    def y_arrive(a, i):
        y_copy(a, i, 1 - y).wait_recv()
        c_copy(a, i, 1, c).start()

    def mirror_go(i, far):
        for a in (0, 1):
            c_copy(a, i, far, 1 - c).wait_recv()
        x_copy(i, far).start()

    def near(a, i):
        z_arrival(a, i).wait_recv()
        c_go(a, i)

    def pass_on(a, i):
        z_arrival(a, i).wait_recv()
        z_copy(a, i + 1).start()
        c_go(a, i)

    def peer_near(i):
        z_arrival(2, i, 1).wait_recv()
        c_go(2, i, 1)

    def peer_pass_on(i):
        z_arrival(2, i, 1).wait_recv()
        z_copy(2, i + 1, 1).start()
        c_go(2, i, 1)

    def tabs_over_y():
        for d in (1, 2, 3):
            tab_z_arrival(d).wait_recv()
        tab_y(y).start()

    def tabs_over_cores():
        tab_y(1 - y).wait_recv()
        tab_c(c).start()

    def peer_begin():
        y_arrive(2, 0)
        z_copy(2, 0, 1).start()

    on_core0 = pl.when(c == 0)
    on_core1 = pl.when(c == 1)
    on_end = pl.when(inner == 0)
    on_middle = pl.when(inner == 1)

    exchange(0).wait_recv()
    for a in (0, 1):
        own(a)
        z_begin(a)
        y_go(a, 0)
        c_go(a, 0)
    exchange(1).wait_recv()
    own(2)
    c_go(2, 0)

    @on_core1
    def _():
        y_go(2, 0)

    @on_middle
    def _():
        pass_on(0, 1)
        y_go(0, 1)
        pass_on(0, 2)
        y_go(0, 2)
        tabs_over_y()
        pass_on(1, 1)
        y_go(1, 1)
        pass_on(1, 2)
        y_go(1, 2)
        z_copy(2, 0).start()
        y_arrive(0, 0)
        y_arrive(1, 0)

        @on_core1
        def _():
            peer_begin()

        pass_on(0, 3)
        y_go(0, 3)
        pass_on(2, 1)

        @on_core1
        def _():
            peer_pass_on(1)

        pass_on(1, 3)
        y_go(1, 3)
        z_copy(2, 1).start()

        @on_core0
        def _():
            y_go(2, 0)
            y_go(2, 1)

        @on_core1
        def _():
            z_copy(2, 1, 1).start()

        mirror_go(0, 0)
        pass_on(2, 2)

        @on_core0
        def _():
            y_go(2, 2)

        @on_core1
        def _():
            peer_pass_on(2)

        mirror_go(1, 0)
        tabs_over_cores()
        y_arrive(0, 1)
        pass_on(2, 3)

        @on_core0
        def _():
            y_go(2, 3)

        @on_core1
        def _():
            peer_pass_on(3)

        mirror_go(0, 1)
        y_arrive(1, 1)
        mirror_go(2, 0)
        y_arrive(0, 2)
        mirror_go(1, 1)
        y_arrive(1, 2)
        mirror_go(3, 0)

    @on_end
    def _():
        z_copy(2, 0).start()
        near(0, 1)
        y_go(0, 1)
        tabs_over_y()
        near(1, 1)
        y_go(1, 1)
        y_arrive(0, 0)
        y_arrive(1, 0)

        @on_core1
        def _():
            peer_begin()

        mirror_go(0, 0)
        near(0, 2)
        y_go(0, 2)
        near(1, 2)
        y_go(1, 2)
        mirror_go(1, 0)
        tabs_over_cores()
        y_arrive(0, 1)
        near(0, 3)
        y_go(0, 3)
        mirror_go(0, 1)
        y_arrive(1, 1)
        near(1, 3)
        y_go(1, 3)

        @on_core0
        def _():
            y_go(2, 0)

        mirror_go(2, 0)
        y_arrive(0, 2)
        mirror_go(1, 1)
        near(2, 1)

        @on_core0
        def _():
            y_go(2, 1)

        @on_core1
        def _():
            peer_near(1)

        y_arrive(1, 2)
        mirror_go(3, 0)

    for load in loads[7:]:
        load.wait()
    tab_c(1 - c).wait_recv()
    for b in range(CHIPS):
        for cc in range(CS):
            at = b * PAIR + cc * TOK
            tab[...] = tabs[cc * CHIPS + b].astype(f32)
            sc[at : at + TOK, :] = tab[0:TOK, :]
    for a in (0, 1):
        y_arrive(a, 3)
    mirror_go(2, 1)
    mirror_go(3, 1)

    def front_step(i):
        if i in (0, 2):
            @on_end
            def _():
                near(2, 2 + i // 2)

                @on_core0
                def _():
                    y_go(2, 2 + i // 2)

                @on_core1
                def _():
                    peer_near(2 + i // 2)

        @on_core0
        def _():
            y_arrive(2, i)

    slot_lanes = lax.broadcasted_iota(jnp.int32, (SLOTS, LANES), 1)

    def scale_of(base):
        return jnp.sum(jnp.where(slot_lanes == k + base, sc[...], 0.0), axis=1, keepdims=True)

    def hidden(a):
        total = None
        for h in range(2):
            parts = []
            for q in range(2):
                at = (2 * h + q) * quarter
                parts += [gate_w[at : at + quarter, :], up_w[at : at + quarter, :]]
            term = nn(xs[a, h], jnp.concatenate(parts, axis=1))
            total = term if total is None else total + term
        total = total.reshape(CHIPS, FOLD, 4 * HID)
        both = total[:, 0:PAIR, 0 : 2 * HID] + total[:, PAIR:, 2 * HID :]
        both = both.reshape(SLOTS, 2 * HID)
        return both[:, 0:HID], both[:, HID:]

    gate, up = hidden(0)
    total = None
    for h in range(2):
        at = 2 * h * quarter
        pair = jnp.concatenate(
            [down_w[:, at : at + quarter], down_w[:, at + quarter : at + 2 * quarter]], axis=0
        )
        term = nt(xs[1, h], pair)
        total = term if total is None else total + term
    total = total.reshape(CHIPS, FOLD, 2 * HID)
    scale = scale_of(0)
    grad = (total[:, 0:PAIR, 0:HID] + total[:, PAIR:, HID:]).reshape(SLOTS, HID) * scale
    sig = 1.0 / (1.0 + jnp.exp(-gate))
    act = gate * sig
    dc[:, 0:HID] = grad * up * (sig * (1.0 + gate * (1.0 - sig)))
    dc[:, HID : 2 * HID] = grad * act
    dc[:, 2 * HID :] = act * up * scale
    dsend[...] = dc[...].astype(bf)
    deltas = remote(dsend, dm, dms.at[0], dms.at[1], mirror)
    deltas.start()
    front_step(0)

    def by_device(width):
        for b in range(CHIPS):
            for cc in range(CS):
                at = b * PAIR + cc * TOK
                to = cc * CHIPS * 16 + b * 16
                r32[to : to + TOK, 0:width] = dc[at : at + TOK, 0:width]
                r32[to + TOK : to + 16, 0:width] = dc[at + 8 : at + TOK, 0:width]
        return r32[:, 0:width].astype(bf)

    drs[...] = by_device(2 * HID)

    def core_sum(a, g):
        j, n = GROUPS[g]
        part = pl.ds(j, n)
        return remote(pb.at[a, 1 - c, part], rc.at[a, part], rs.at[a, g, 0], rr.at[a, g, 0], core_dev)

    def y_sum(a, g):
        j, n = GROUPS[g]
        part = pl.ds(j, n)
        rows = pl.ds(pl.multiple_of((1 - y) * ZS * FOLD, 16), ZS * FOLD)
        return remote(pb.at[a, c, part, rows], ry.at[a, part], rs.at[a, g, 4], rr.at[a, g, 4], y_dev)

    def z_sum(a, g, d):
        j, n = GROUPS[g]
        part = pl.ds(j, n)
        rows = pl.ds(pl.multiple_of(zpeer[d] * FOLD, 16), FOLD)
        return remote(zsb.at[a, part, rows], rz.at[a, d - 1, part], rs.at[a, g, d], rr.at[a, g, d], z_dev[d])

    early = lax.broadcasted_iota(jnp.int32, (1, 1, 8, 1), 2) < 4

    def part(a, g):
        j, n = GROUPS[g]
        wide_of = n * LANES
        outs = []
        for q in range(4):
            at = q * quarter + j * LANES
            if a == 0:
                both = jnp.concatenate([gate_w[at : at + wide_of, :], up_w[at : at + wide_of, :]], axis=1)
                out = nt(drs[...], both)
            else:
                out = nn(ers[...], down_w[:, at : at + wide_of])
            outs.append(out.reshape(CS, CHIPS, 16, wide_of))
        tops = [out[:, :, 0:8] for out in outs]
        ends = [jnp.where(early, outs[2 * i][:, :, 8:16], outs[2 * i + 1][:, :, 8:16]) for i in range(2)]
        folded = jnp.concatenate(tops + ends, axis=2).reshape(CS, DEPTH, wide_of).astype(bf)
        for i in range(n):
            pb[a, :, j + i] = folded[:, :, i * LANES : (i + 1) * LANES]
        core_sum(a, g).start()

    def over_cores(a, g):
        j, n = GROUPS[g]
        part = pl.ds(j, n)
        core_sum(a, g).wait_recv()
        for yy in (1 - y, y):
            rows = pl.ds(pl.multiple_of(yy * ZS * FOLD, 16), ZS * FOLD)
            pb[a, c, part, rows, :] = (
                pb[a, c, part, rows, :].astype(f32) + rc[a, part, rows, :].astype(f32)
            ).astype(bf)
            if yy is not y:
                y_sum(a, g).start()

    def over_y(a, g):
        j, n = GROUPS[g]
        part = pl.ds(j, n)
        y_sum(a, g).wait_recv()
        rows = pl.ds(pl.multiple_of(y * ZS * FOLD, 16), ZS * FOLD)
        zsb[a, part] = (pb[a, c, part, rows, :].astype(f32) + ry[a, part].astype(f32)).astype(bf)
        for d in (1, 2, 3):
            z_sum(a, g, d).start()

    def over_z(a, g, out):
        j, n = GROUPS[g]
        part = pl.ds(j, n)
        rows = pl.ds(pl.multiple_of(z * FOLD, 16), FOLD)
        total = zsb[a, part, rows, :].astype(f32)
        for d in (1, 2, 3):
            z_sum(a, g, d).wait_recv()
            total = total + rz[a, d - 1, part].astype(f32)
        tot[part] = total
        for i in range(n):
            for q in range(4):
                piece = jnp.concatenate(
                    [tot[j + i, 8 * q : 8 * q + 8], tot[j + i, 32 + 4 * q : 36 + 4 * q]], axis=0
                )
                at = q * quarter + (j + i) * LANES
                out[:, at : at + LANES] = piece.astype(bf)

    part(0, 0)
    front_step(1)
    part(0, 1)
    over_cores(0, 0)
    front_step(2)
    part(0, 2)
    over_cores(0, 1)
    front_step(3)
    over_cores(0, 2)
    for far in (0, 1):
        for i in range(4):
            c_copy(2, i, far, 1 - c).wait_recv()
    gate, up = hidden(2)
    dc[:, 0:HID] = gate / (1.0 + jnp.exp(-gate)) * up * scale_of(EXPERTS)
    ers[...] = by_device(HID)
    part(1, 0)
    over_y(0, 0)
    part(1, 1)
    over_cores(1, 0)
    over_y(0, 1)
    part(1, 2)
    over_cores(1, 1)
    for far in (0, 1):
        for i in range(4):
            x_copy(i, far).wait_recv()
        m_copy(far, c).start()
    over_y(0, 2)
    over_cores(1, 2)
    over_z(0, 0, back_out)
    deltas.wait_recv()

    def spread(rows):
        rows = rows.reshape(CHIPS, PAIR, 3 * HID)
        pair, last = rows[:, :, 0 : 2 * HID], rows[:, :, 2 * HID :]
        empty, short = jnp.zeros_like(pair), jnp.zeros_like(last)
        first = jnp.concatenate([pair, empty, last, short], axis=2)
        second = jnp.concatenate([empty, pair, short, last], axis=2)
        return jnp.concatenate([first, second], axis=1).reshape(DEPTH, 6 * HID).astype(bf)

    de[0:DEPTH, :] = spread(dsend[...].astype(f32))
    de[DEPTH:, :] = spread(dm[...].astype(f32))
    over_y(1, 0)
    for far in (0, 1):
        m_copy(far, 1 - c).wait_recv()

    def grads(g):
        j, n = GROUPS[g]
        cols = slice(j * LANES, (j + n) * LANES)
        size = n * LANES
        both = tn(jnp.concatenate([xs[0, pipe, :, cols], ms[0, :, cols]], axis=0), de[:, 0 : 4 * HID]).astype(bf)
        last = tn(de[:, 4 * HID :], jnp.concatenate([xs[1, pipe, :, cols], ms[1, :, cols]], axis=0)).astype(bf)
        for q in range(2):
            at = q * quarter + j * LANES
            gate_out[at : at + size, :] = both[:, 2 * q * HID : (2 * q + 1) * HID]
            up_out[at : at + size, :] = both[:, (2 * q + 1) * HID : (2 * q + 2) * HID]
            dn_out[:, at : at + size] = last[q * HID : (q + 1) * HID]

    grads(0)
    over_z(0, 1, back_out)
    over_y(1, 1)
    grads(1)
    over_z(0, 2, back_out)
    over_y(1, 2)
    grads(2)
    for g in range(len(GROUPS)):
        over_z(1, g, front_out)

    for i in (0, 1):
        exchange(i).wait_send()
    def z_drain(a, far):
        z_copy(a, 0, far).wait_send()

        @pl.when(inner == 1)
        def _():
            for slot in range(1, 5):
                z_copy(a, slot, far).wait_send()

    for a in range(3):
        z_drain(a, 0)
        for i in range(4):
            if i == 0 or a < 2:
                y_copy(a, i, y).wait_send()
            for far in (0, 1):
                c_copy(a, i, far, c).wait_send()

    @pl.when(c == 0)
    def _():
        for i in range(1, 4):
            y_copy(2, i, y).wait_send()

    @pl.when(c == 1)
    def _():
        z_drain(2, 1)

    for far in (0, 1):
        for i in range(4):
            x_copy(i, far).wait_send()
        m_copy(far, c).wait_send()
    for d in (1, 2, 3):
        tab_z(d).wait_send()
    tab_y(y).wait_send()
    tab_c(c).wait_send()
    deltas.wait_send()
    for a in range(2):
        for g in range(len(GROUPS)):
            core_sum(a, g).wait_send()
            y_sum(a, g).wait_send()
            for d in (1, 2, 3):
                z_sum(a, g, d).wait_send()


def place(*refs):
    count = len(refs) // 2
    for i in range(count):
        refs[count + i][...] = refs[i][...]


def local_kernel(
    front_tokens, front_routes, front_mixing, back_tokens, back_routes, back_mixing,
    back_upstream, gate_weight, up_weight, down_weight,
):
    features = front_tokens.shape[2]
    half = features // 2
    quarter = features // 4
    tiles = quarter // LANES
    bf, f32 = jnp.bfloat16, jnp.float32
    vm = pltpu.VMEM
    dma = pltpu.SemaphoreType.DMA
    results = pl.pallas_call(
        functools.partial(kernel, features),
        out_shape=[
            pltpu.VMEM((TOK, features), bf),
            pltpu.VMEM((TOK, features), bf),
            pltpu.VMEM((half, HID), bf),
            pltpu.VMEM((half, HID), bf),
            pltpu.VMEM((HID, half), bf),
        ],
        in_specs=[pl.BlockSpec(memory_space=pltpu.MemorySpace.HBM)] * 10,
        out_specs=[pl.BlockSpec(memory_space=vm)] * 5,
        scratch_shapes=[
            vm((3, TOK, features), bf),
            vm((4, TOP, TOK), jnp.int32),
            vm((features, HID), bf),
            vm((features, HID), bf),
            vm((HID, features), bf),
            vm((3, 2, FOLD, quarter), f32),
            vm((3, FOLD, quarter), bf),
            vm((3, FOLD, quarter), bf),
            vm((3, 2, DEPTH, quarter), bf),
            vm((2, DEPTH, quarter), bf),
            vm((16, LANES), f32),
            vm((BLOCKS, 16, LANES), bf),
            vm((SLOTS, LANES), f32),
            vm((SLOTS, 3 * HID), f32),
            vm((SLOTS, 3 * HID), bf),
            vm((SLOTS, 3 * HID), bf),
            vm((2 * DEPTH, 6 * HID), bf),
            vm((BLOCKS * 16, 2 * HID), f32),
            vm((BLOCKS * 16, 2 * HID), bf),
            vm((BLOCKS * 16, HID), bf),
            vm((2, CS, tiles, DEPTH, LANES), bf),
            vm((2, tiles, DEPTH, LANES), bf),
            vm((2, tiles, ZS * FOLD, LANES), bf),
            vm((2, tiles, ZS * FOLD, LANES), bf),
            vm((2, ZS - 1, tiles, FOLD, LANES), bf),
            vm((tiles, FOLD, LANES), f32),
            dma((10,)), dma((2, 2)),
            dma((4, 5)), dma((4, 3)), dma((3, 4)), dma((3, 4)), dma((3, 8)), dma((3, 8)),
            dma((8,)), dma((8,)), dma((2,)), dma((2,)), dma((5,)), dma((5,)), dma((2,)),
            dma((2, len(GROUPS), 5)), dma((2, len(GROUPS), 5)),
        ],
        compiler_params=pltpu.CompilerParams(
            collective_id=0, has_side_effects=True, vmem_limit_bytes=VMEM_LIMIT
        ),
    )(
        back_tokens[0], back_upstream[0], front_tokens[0], back_routes[0].T, back_mixing[0].T,
        front_routes[0].T, front_mixing[0].T, gate_weight[0], up_weight[0], down_weight[0],
    )
    front, back, gate, up, down = pl.pallas_call(
        place,
        out_shape=[jax.ShapeDtypeStruct(item.shape, item.dtype) for item in results],
        in_specs=[pl.BlockSpec(memory_space=vm)] * 5,
        out_specs=[pl.BlockSpec(memory_space=vm)] * 5,
        compiler_params=pltpu.CompilerParams(vmem_limit_bytes=8 * 1024 * 1024),
    )(*results)
    return front[None], back[None], gate[None], up[None], down[None]


def solution(mesh):
    fits = mesh.shape["pipe"] == 2 and mesh.shape["expert"] == BLOCKS
    local = local_kernel if fits else local_collectives
    rows = P("pipe", "expert", None)
    columns = P("pipe", None, "expert")
    return jax.shard_map(
        local,
        mesh=mesh,
        in_specs=(rows,) * 7 + (columns, columns, rows),
        out_specs=(rows, rows, columns, columns, rows),
        check_vma=False,
    )
```

```python
import functools

import jax
import jax.numpy as jnp
from jax import lax
from jax.experimental import pallas as pl
from jax.experimental.pallas import tpu as pltpu
from jax.sharding import PartitionSpec as P

SHARDS = 8
LANES = 128
TOP = 2

weight_unit = 0.0625


def token_weights(routes, mixing):
    hits = routes[:, :, None] == jnp.arange(LANES, dtype=jnp.int32)[None, None, :]
    weights = mixing.astype(jnp.float32) * weight_unit
    return jnp.sum(jnp.where(hits, weights[:, :, None], 0.0), axis=1).astype(jnp.bfloat16)


def rows_dot(rows, matrix, dim):
    return lax.dot_general(
        rows, matrix, (((2,), (dim,)), ((), ())), preferred_element_type=jnp.float32
    )


def grad_dot(rows, deltas):
    return lax.dot_general(
        rows, deltas, (((0, 1), (0, 1)), ((), ())), preferred_element_type=jnp.float32
    ).astype(jnp.bfloat16)


def local_collectives(
    front_tokens,
    front_routes,
    front_mixing,
    back_tokens,
    back_routes,
    back_mixing,
    back_upstream,
    gate_weight,
    up_weight,
    down_weight,
):
    tokens = front_tokens.shape[1]
    features = front_tokens.shape[2]
    gate_cols = gate_weight[0]
    up_cols = up_weight[0]
    down_rows = down_weight[0]
    expert = lax.axis_index("expert") // SHARDS
    picked = (jnp.arange(LANES, dtype=jnp.int32) == expert).astype(jnp.float32)

    front_table = token_weights(front_routes[0], front_mixing[0])
    back_table = token_weights(back_routes[0], back_mixing[0])
    back_load = jnp.concatenate(
        [
            jnp.concatenate([back_tokens[0], jnp.zeros_like(back_table)], axis=1),
            jnp.concatenate([back_upstream[0], back_table], axis=1),
        ],
        axis=0,
    )
    front_load = jnp.concatenate([front_tokens[0], front_table], axis=1)
    back_all = lax.all_gather(back_load, "expert", axis=0)
    front_all = lax.all_gather(front_load, "expert", axis=0)

    def own_weight(table):
        return jnp.sum(table.astype(jnp.float32) * picked, axis=2, keepdims=True)

    back_rows = back_all[:, :tokens, :features]
    upstream = back_all[:, tokens:, :features]
    back_scale = own_weight(back_all[:, tokens:, features:])
    scaled_rows = (upstream.astype(jnp.float32) * back_scale).astype(jnp.bfloat16)
    back_gate = rows_dot(back_rows, gate_cols, 0)
    back_up = rows_dot(back_rows, up_cols, 0)
    hidden_grad = rows_dot(scaled_rows, down_rows, 1)
    gate_sig = jax.nn.sigmoid(back_gate)
    gate_act = back_gate * gate_sig
    back_hidden = (gate_act * back_up).astype(jnp.bfloat16)
    act_slope = gate_sig * (1.0 + back_gate * (1.0 - gate_sig))
    gate_delta = (hidden_grad * back_up * act_slope).astype(jnp.bfloat16)
    up_delta = (hidden_grad * gate_act).astype(jnp.bfloat16)
    sections = jnp.stack(
        [
            grad_dot(back_rows, gate_delta),
            grad_dot(back_rows, up_delta),
            grad_dot(scaled_rows, back_hidden),
        ]
    )
    pipe_count = lax.axis_size("pipe")
    half = features // 2
    upper = lax.axis_index("pipe") * 2 >= pipe_count
    own_start = jnp.where(upper, half, 0)
    own_half = lax.dynamic_slice_in_dim(sections, own_start, half, axis=1)
    leaving = lax.dynamic_slice_in_dim(sections, half - own_start, half, axis=1)
    arrived = lax.ppermute(leaving, "pipe", [(p, pipe_count - 1 - p) for p in range(pipe_count)])

    back_parts = (rows_dot(gate_delta, gate_cols, 1) + rows_dot(up_delta, up_cols, 1)).astype(
        jnp.bfloat16
    )
    front_rows = front_all[:, :, :features]
    front_scale = own_weight(front_all[:, :, features:])
    front_gate = rows_dot(front_rows, gate_cols, 0)
    front_up = rows_dot(front_rows, up_cols, 0)
    front_hidden = (jax.nn.silu(front_gate) * front_up).astype(jnp.bfloat16)
    front_parts = (rows_dot(front_hidden, down_rows, 0) * front_scale).astype(jnp.bfloat16)
    totals = lax.psum_scatter(
        jnp.concatenate([front_parts, back_parts], axis=1), "expert", scatter_dimension=0
    )
    summed = (own_half.astype(jnp.float32) + arrived.astype(jnp.float32)).astype(jnp.bfloat16)
    return (
        totals[:tokens][None],
        totals[tokens:][None],
        summed[0][None],
        summed[1][None],
        summed[2].T[None],
    )


MESH = pl.DeviceIdType.MESH
TOK = 12
EXPERTS = 2
ZS, YS, CS = 4, 2, 2
CHIPS = ZS * YS
BLOCKS = CHIPS * CS
HID = 128
PAIR = 2 * TOK
FOLD = 2 * PAIR
DEPTH = CHIPS * FOLD
SLOTS = CHIPS * PAIR
GROUPS = ((0, 2), (2, 2), (4, 3))
PIECES = ((0, 2), (2, 2), (4, 3))
VMEM_LIMIT = 61 * 1024 * 1024


def nn(a, b):
    return jnp.dot(a, b, preferred_element_type=jnp.float32)


def nt(a, b):
    return lax.dot_general(a, b, (((1,), (1,)), ((), ())), preferred_element_type=jnp.float32)


def tn(a, b):
    return lax.dot_general(a, b, (((0,), (0,)), ((), ())), preferred_element_type=jnp.float32)


def kernel(
    features,
    back_hbm, up_hbm, front_hbm, broutes_hbm, bmix_hbm, froutes_hbm, fmix_hbm, gate_hbm, up_w_hbm, down_hbm,
    front_out, back_out, gate_out, up_out, dn_out,
    stage, mix, gate_w, up_w, down_w, wide, ex_send, ex_recv, xs, ms, tab, tabs, sc, dc, dsend, dm, de,
    r32, drs, ers, pb, rc, ry, zsb, rz, tot,
    local_sems, ex_sems, zs, zr, ys, yr, cs, cr, xsem, xrem, mcs, mcr, ts, tr, dms, rs, rr,
):
    f32, bf = jnp.float32, jnp.bfloat16
    me = lax.axis_index("expert")
    pipe = lax.axis_index("pipe")
    c = me % CS
    y = (me // CS) % YS
    z = me // (CS * YS)
    k = me // SHARDS
    quarter = features // 4
    half = features // 2

    def dev(zz, yy, cc):
        return {"expert": (zz * YS + yy) * CS + cc}

    zpeer = [None] + [(z + d) % ZS for d in range(1, ZS)]
    zfrom = [None] + [(z + ZS - d) % ZS for d in range(1, ZS)]
    core_dev = dev(z, y, 1 - c)
    y_dev = dev(z, 1 - y, c)
    z_dev = [None] + [dev(zpeer[d], y, c) for d in range(1, ZS)]
    mirror = {"pipe": 1 - pipe}
    low = z < 2
    inner = jnp.where(low, z, 3 - z)

    def real(s):
        return jnp.where(low, s, 3 - s)

    sources = [z, real(1 - inner), real(2), real(3)]
    z_in = dev(real(1 + inner), y, c)
    z_out = dev(real(0), y, c)

    loads = [
        pltpu.make_async_copy(src, dst, local_sems.at[i])
        for i, (src, dst) in enumerate(
            [
                (back_hbm, stage.at[0]), (up_hbm, stage.at[1]), (front_hbm, stage.at[2]),
                (froutes_hbm, mix.at[0]), (fmix_hbm, mix.at[1]), (broutes_hbm, mix.at[2]), (bmix_hbm, mix.at[3]),
                (gate_hbm, gate_w), (up_w_hbm, up_w), (down_hbm, down_w),
            ]
        )
    ]
    for load in loads:
        load.start()

    barrier = pltpu.get_barrier_semaphore()
    for target in [core_dev, y_dev, z_dev[1], z_dev[2], z_dev[3], mirror]:
        pl.semaphore_signal(barrier, inc=1, device_id=target, device_id_type=MESH)

    lanes = lax.broadcasted_iota(jnp.int32, (TOK, LANES), 1)
    square = (TOK, TOK)
    diagonal = lax.broadcasted_iota(jnp.int32, square, 0) == lax.broadcasted_iota(jnp.int32, square, 1)

    def upright(row):
        wide_row = jnp.broadcast_to(row.astype(f32), square)
        return jnp.sum(jnp.where(diagonal, wide_row, 0.0), axis=1, keepdims=True)

    def table(routes, mixing, base):
        out = jnp.zeros((TOK, LANES), f32)
        for j in range(TOP):
            weight = upright(mixing[j : j + 1]) * weight_unit
            out = out + jnp.where(upright(routes[j : j + 1]).astype(jnp.int32) + base == lanes, weight, 0.0)
        return out

    chip = y * ZS + z
    own_tab = c * CHIPS + chip

    for load in loads[:7]:
        load.wait()
    for a in range(3):
        rows = stage[a].astype(f32)
        for h in range(2):
            for q in range(2):
                at = (2 * h + q) * quarter
                piece = rows[:, at : at + quarter]
                for cc in range(2):
                    top = q * PAIR + cc * TOK
                    wide[a, h, top : top + TOK, :] = jnp.where(c == cc, piece, 0.0)
    for a in range(3):
        ex_send[a] = wide[a, 1 - c].astype(bf)
    tab[...] = jnp.zeros_like(tab)
    tab[0:TOK, :] = table(mix[2], mix[3], 0) + table(mix[0], mix[1], EXPERTS)
    tabs[own_tab] = tab[...].astype(bf)
    pl.semaphore_wait(barrier, 6)

    def remote(src, dst, ssem, rsem, target):
        return pltpu.make_async_remote_copy(
            src_ref=src, dst_ref=dst, send_sem=ssem, recv_sem=rsem,
            device_id=target, device_id_type=MESH,
        )

    def exchange(i):
        part = pl.ds(0, 2) if i == 0 else pl.ds(2, 1)
        return remote(ex_send.at[part], ex_recv.at[part], ex_sems.at[0, i], ex_sems.at[1, i], core_dev)

    exchange(0).start()
    exchange(1).start()

    def tab_z(d):
        return remote(tabs.at[own_tab], tabs.at[own_tab], ts.at[1], tr.at[1], z_dev[d])

    some = tabs.at[pl.ds(0, ZS - 1)]
    three_tabs = remote(some, some, ts.at[1], tr.at[1], z_dev[1])

    def tab_y(yy):
        part = tabs.at[pl.ds(c * CHIPS + yy * ZS, ZS)]
        return remote(part, part, ts.at[0], tr.at[0], y_dev)

    def tab_c(cc):
        part = tabs.at[pl.ds(cc * CHIPS, CHIPS)]
        return remote(part, part, ts.at[2], tr.at[2], core_dev)

    for d in (1, 2, 3):
        tab_z(d).start()

    def rows_of(zz, yy):
        return pl.ds(pl.multiple_of((yy * ZS + zz) * FOLD, 16), FOLD)

    def block(a, h, zz, yy):
        return xs.at[a, h, rows_of(zz, yy)]

    def z_copy(a, slot, far=0):
        yy = 1 - y if far else y
        own_at = block(a, c, z, yy)
        if slot == 0:
            return remote(own_at, own_at, zs.at[far], zr.at[a + far, inner], z_in)
        if slot == 1:
            return remote(own_at, own_at, zs.at[far], zr.at[a + far, 0], z_out)
        i = slot - 1
        at = block(a, c, sources[i], yy)
        target, arrival = (z_in, 2) if i == 1 else (z_out, i - 1)
        return remote(at, at, zs.at[far], zr.at[a + far, arrival], target)

    def z_arrival(a, i, far=0):
        at = block(a, c, sources[i], 1 - y if far else y)
        return remote(at, at, zs.at[far], zr.at[a + far, i - 1], z_in)

    def y_copy(a, i, yy):
        at = block(a, c, sources[i], yy)
        return remote(at, at, ys.at[a // 2], yr.at[a, i], y_dev)

    def c_copy(a, i, far, cc):
        at = block(a, cc, sources[i], 1 - y if far else y)
        return remote(at, at, cs.at[0], cr.at[8 * a + 4 * far + i if a < 2 else 16], core_dev)

    def x_copy(i, far):
        rows = rows_of(sources[i], 1 - y if far else y)
        return remote(xs.at[c, 1 - pipe, rows], ms.at[c, rows], xsem.at[0], xrem.at[far], mirror)

    def x_group(far):
        yy = 1 - y if far else y
        rows = pl.ds(pl.multiple_of(yy * ZS * FOLD, 16), ZS * FOLD)
        return remote(xs.at[c, 1 - pipe, rows], ms.at[c, rows], xsem.at[0], xrem.at[far], mirror)

    def m_copy(far, cc):
        yy = 1 - y if far else y
        rows = pl.ds(pl.multiple_of(yy * ZS * FOLD, 16), ZS * FOLD)
        return remote(ms.at[cc, rows], ms.at[cc, rows], mcs.at[far], mcr.at[far], core_dev)

    def own(a):
        xs[a, c, rows_of(z, y), :] = (wide[a, c] + ex_recv[a].astype(f32)).astype(bf)

    def z_begin(a, far=0):
        z_copy(a, 0, far).start()

        @pl.when(inner == 1)
        def _():
            z_copy(a, 1, far).start()

    def z_arrive(a, i, far=0):
        z_arrival(a, i, far).wait_recv()

        @pl.when(inner == 1)
        def _():
            z_copy(a, i + 1, far).start()

    def y_go(a, i):
        y_copy(a, i, y).start()

    def c_go(a, i, far=0):
        c_copy(a, i, far, c).start()

    def y_arrive(a, i):
        y_copy(a, i, 1 - y).wait_recv()
        c_copy(a, i, 1, c).start()

    def mirror_go(i, far):
        for a in (0, 1):
            c_copy(a, i, far, 1 - c).wait_recv()
        x_copy(i, far).start()

    def near(a, i):
        z_arrival(a, i).wait_recv()
        c_go(a, i)

    def pass_on(a, i):
        z_arrival(a, i).wait_recv()
        z_copy(a, i + 1).start()
        c_go(a, i)

    def peer_near(i):
        z_arrival(2, i, 1).wait_recv()
        c_go(2, i, 1)

    def peer_pass_on(i):
        z_arrival(2, i, 1).wait_recv()
        z_copy(2, i + 1, 1).start()
        c_go(2, i, 1)

    def tabs_over_y():
        three_tabs.wait_recv()
        tab_y(y).start()

    def tabs_over_cores():
        tab_y(1 - y).wait_recv()
        tab_c(c).start()

    def peer_begin():
        y_arrive(2, 0)
        z_copy(2, 0, 1).start()

    on_core0 = pl.when(c == 0)
    on_core1 = pl.when(c == 1)
    on_end = pl.when(inner == 0)
    on_middle = pl.when(inner == 1)

    exchange(0).wait_recv()
    for a in (0, 1):
        own(a)
        z_begin(a)
        y_go(a, 0)
        c_go(a, 0)
    exchange(1).wait_recv()
    own(2)
    c_go(2, 0)

    @on_core1
    def _():
        y_go(2, 0)

    @on_middle
    def _():
        pass_on(0, 1)
        y_go(0, 1)
        pass_on(0, 2)
        y_go(0, 2)
        tabs_over_y()
        pass_on(1, 1)
        y_go(1, 1)
        pass_on(1, 2)
        y_go(1, 2)
        z_copy(2, 0).start()
        y_arrive(0, 0)
        y_arrive(1, 0)

        @on_core1
        def _():
            peer_begin()

        pass_on(0, 3)
        y_go(0, 3)
        pass_on(2, 1)

        @on_core1
        def _():
            peer_pass_on(1)

        pass_on(1, 3)
        y_go(1, 3)
        z_copy(2, 1).start()

        @on_core0
        def _():
            y_go(2, 0)
            y_go(2, 1)

        @on_core1
        def _():
            z_copy(2, 1, 1).start()

        mirror_go(0, 0)
        pass_on(2, 2)

        @on_core0
        def _():
            y_go(2, 2)

        @on_core1
        def _():
            peer_pass_on(2)

        mirror_go(1, 0)
        tabs_over_cores()
        y_arrive(0, 1)
        pass_on(2, 3)

        @on_core0
        def _():
            y_go(2, 3)

        @on_core1
        def _():
            peer_pass_on(3)

        mirror_go(0, 1)
        y_arrive(1, 1)
        mirror_go(2, 0)
        y_arrive(0, 2)
        mirror_go(1, 1)
        y_arrive(1, 2)
        mirror_go(3, 0)

    @on_end
    def _():
        z_copy(2, 0).start()
        near(0, 1)
        y_go(0, 1)
        tabs_over_y()
        near(1, 1)
        y_go(1, 1)
        y_arrive(0, 0)
        y_arrive(1, 0)

        @on_core1
        def _():
            peer_begin()

        mirror_go(0, 0)
        near(0, 2)
        y_go(0, 2)
        near(1, 2)
        y_go(1, 2)
        mirror_go(1, 0)
        tabs_over_cores()
        y_arrive(0, 1)
        near(0, 3)
        y_go(0, 3)
        mirror_go(0, 1)
        y_arrive(1, 1)
        near(1, 3)
        y_go(1, 3)

        @on_core0
        def _():
            y_go(2, 0)

        mirror_go(2, 0)
        y_arrive(0, 2)
        mirror_go(1, 1)
        near(2, 1)

        @on_core0
        def _():
            y_go(2, 1)

        @on_core1
        def _():
            peer_near(1)

        y_arrive(1, 2)
        mirror_go(3, 0)

    for load in loads[7:]:
        load.wait()
    tab_c(1 - c).wait_recv()
    for b in range(CHIPS):
        for cc in range(CS):
            at = b * PAIR + cc * TOK
            tab[...] = tabs[cc * CHIPS + b].astype(f32)
            sc[at : at + TOK, :] = tab[0:TOK, :]
    for a in (0, 1):
        y_arrive(a, 3)
    mirror_go(2, 1)
    mirror_go(3, 1)

    def front_step(i):
        if i in (0, 2):
            @on_end
            def _():
                near(2, 2 + i // 2)

                @on_core0
                def _():
                    y_go(2, 2 + i // 2)

                @on_core1
                def _():
                    peer_near(2 + i // 2)

        @on_core0
        def _():
            y_arrive(2, i)

    slot_lanes = lax.broadcasted_iota(jnp.int32, (SLOTS, LANES), 1)

    def scale_of(base):
        return jnp.sum(jnp.where(slot_lanes == k + base, sc[...], 0.0), axis=1, keepdims=True)

    def hidden(a):
        total = None
        for h in range(2):
            parts = []
            for q in range(2):
                at = (2 * h + q) * quarter
                parts += [gate_w[at : at + quarter, :], up_w[at : at + quarter, :]]
            term = nn(xs[a, h], jnp.concatenate(parts, axis=1))
            total = term if total is None else total + term
        total = total.reshape(CHIPS, FOLD, 4 * HID)
        both = total[:, 0:PAIR, 0 : 2 * HID] + total[:, PAIR:, 2 * HID :]
        both = both.reshape(SLOTS, 2 * HID)
        return both[:, 0:HID], both[:, HID:]

    gate, up = hidden(0)
    total = None
    for h in range(2):
        at = 2 * h * quarter
        pair = jnp.concatenate(
            [down_w[:, at : at + quarter], down_w[:, at + quarter : at + 2 * quarter]], axis=0
        )
        term = nt(xs[1, h], pair)
        total = term if total is None else total + term
    total = total.reshape(CHIPS, FOLD, 2 * HID)
    scale = scale_of(0)
    grad = (total[:, 0:PAIR, 0:HID] + total[:, PAIR:, HID:]).reshape(SLOTS, HID) * scale
    sig = 1.0 / (1.0 + jnp.exp(-gate))
    act = gate * sig
    dc[:, 0:HID] = grad * up * (sig * (1.0 + gate * (1.0 - sig)))
    dc[:, HID : 2 * HID] = grad * act
    dc[:, 2 * HID :] = act * up * scale
    dsend[...] = dc[...].astype(bf)
    deltas = remote(dsend, dm, dms.at[0], dms.at[1], mirror)
    deltas.start()
    front_step(0)

    def by_device(width):
        for b in range(CHIPS):
            for cc in range(CS):
                at = b * PAIR + cc * TOK
                to = cc * CHIPS * 16 + b * 16
                r32[to : to + TOK, 0:width] = dc[at : at + TOK, 0:width]
                r32[to + TOK : to + 16, 0:width] = dc[at + 8 : at + TOK, 0:width]
        return r32[:, 0:width].astype(bf)

    drs[...] = by_device(2 * HID)

    def core_sum(a, g):
        j, n = GROUPS[g]
        part = pl.ds(j, n)
        return remote(pb.at[a, 1 - c, part], rc.at[a, part], rs.at[a, 0], rr.at[a, g, 0], core_dev)

    def y_sum(a, g):
        j, n = GROUPS[g]
        part = pl.ds(j, n)
        rows = pl.ds(pl.multiple_of((1 - y) * ZS * FOLD, 16), ZS * FOLD)
        return remote(pb.at[a, c, part, rows], ry.at[a, part], rs.at[a, 1], rr.at[a, g, 1], y_dev)

    def z_sum(a, g, d):
        j, n = GROUPS[g]
        part = pl.ds(j, n)
        rows = pl.ds(pl.multiple_of(zpeer[d] * FOLD, 16), FOLD)
        return remote(zsb.at[a, part, rows], rz.at[a, d - 1, part], rs.at[a, 2], rr.at[a, g, 2], z_dev[d])

    early = lax.broadcasted_iota(jnp.int32, (1, 1, 8, 1), 2) < 4

    def part(a, g):
        j, n = GROUPS[g]
        wide_of = n * LANES
        outs = []
        for q in range(4):
            at = q * quarter + j * LANES
            if a == 0:
                both = jnp.concatenate([gate_w[at : at + wide_of, :], up_w[at : at + wide_of, :]], axis=1)
                out = nt(drs[...], both)
            else:
                out = nn(ers[...], down_w[:, at : at + wide_of])
            outs.append(out.reshape(CS, CHIPS, 16, wide_of))
        tops = [out[:, :, 0:8] for out in outs]
        ends = [jnp.where(early, outs[2 * i][:, :, 8:16], outs[2 * i + 1][:, :, 8:16]) for i in range(2)]
        folded = jnp.concatenate(tops + ends, axis=2).reshape(CS, DEPTH, wide_of).astype(bf)
        for i in range(n):
            pb[a, :, j + i] = folded[:, :, i * LANES : (i + 1) * LANES]
        core_sum(a, g).start()

    def over_cores(a, g):
        j, n = GROUPS[g]
        part = pl.ds(j, n)
        core_sum(a, g).wait_recv()
        for yy in (1 - y, y):
            rows = pl.ds(pl.multiple_of(yy * ZS * FOLD, 16), ZS * FOLD)
            pb[a, c, part, rows, :] = (
                pb[a, c, part, rows, :].astype(f32) + rc[a, part, rows, :].astype(f32)
            ).astype(bf)
            if yy is not y:
                y_sum(a, g).start()

    def over_y(a, g):
        j, n = GROUPS[g]
        part = pl.ds(j, n)
        y_sum(a, g).wait_recv()
        rows = pl.ds(pl.multiple_of(y * ZS * FOLD, 16), ZS * FOLD)
        zsb[a, part] = (pb[a, c, part, rows, :].astype(f32) + ry[a, part].astype(f32)).astype(bf)
        for d in (1, 2, 3):
            z_sum(a, g, d).start()

    def over_z(a, g, out):
        j, n = GROUPS[g]
        part = pl.ds(j, n)
        rows = pl.ds(pl.multiple_of(z * FOLD, 16), FOLD)
        arrived = rz.at[a, :, part]
        remote(arrived, arrived, rs.at[a, 2], rr.at[a, g, 2], y_dev).wait_recv()
        total = zsb[a, part, rows, :].astype(f32)
        for d in (1, 2, 3):
            total = total + rz[a, d - 1, part].astype(f32)
        tot[part] = total
        for i in range(n):
            for q in range(4):
                piece = jnp.concatenate(
                    [tot[j + i, 8 * q : 8 * q + 8], tot[j + i, 32 + 4 * q : 36 + 4 * q]], axis=0
                )
                at = q * quarter + (j + i) * LANES
                out[:, at : at + LANES] = piece.astype(bf)

    last = len(GROUPS) - 1
    for g in range(last + 1):
        part(0, g)
        if g < 3:
            front_step(g + 1)
        if g:
            over_cores(0, g - 1)
    for g in range(last + 1, 3):
        front_step(g + 1)
    over_cores(0, last)
    every = xs.at[2, 1 - c]
    remote(every, every, cs.at[0], cr.at[16], core_dev).wait_recv()
    gate, up = hidden(2)
    dc[:, 0:HID] = gate / (1.0 + jnp.exp(-gate)) * up * scale_of(EXPERTS)
    ers[...] = by_device(HID)
    for g in range(last + 1):
        part(1, g)
        if g:
            over_cores(1, g - 1)
        over_y(0, g)
    over_cores(1, last)
    for far in (0, 1):
        x_group(far).wait_recv()
        m_copy(far, c).start()
    over_z(0, 0, back_out)
    deltas.wait_recv()

    def spread(rows):
        rows = rows.reshape(CHIPS, PAIR, 3 * HID)
        pair, last = rows[:, :, 0 : 2 * HID], rows[:, :, 2 * HID :]
        empty, short = jnp.zeros_like(pair), jnp.zeros_like(last)
        first = jnp.concatenate([pair, empty, last, short], axis=2)
        second = jnp.concatenate([empty, pair, short, last], axis=2)
        return jnp.concatenate([first, second], axis=1).reshape(DEPTH, 6 * HID).astype(bf)

    de[0:DEPTH, :] = spread(dsend[...].astype(f32))
    de[DEPTH:, :] = spread(dm[...].astype(f32))
    over_y(1, 0)
    for far in (0, 1):
        m_copy(far, 1 - c).wait_recv()

    def grads(g):
        j, n = PIECES[g]
        cols = slice(j * LANES, (j + n) * LANES)
        size = n * LANES
        both = tn(jnp.concatenate([xs[0, pipe, :, cols], ms[0, :, cols]], axis=0), de[:, 0 : 4 * HID]).astype(bf)
        last = tn(de[:, 4 * HID :], jnp.concatenate([xs[1, pipe, :, cols], ms[1, :, cols]], axis=0)).astype(bf)
        for q in range(2):
            at = q * quarter + j * LANES
            gate_out[at : at + size, :] = both[:, 2 * q * HID : (2 * q + 1) * HID]
            up_out[at : at + size, :] = both[:, (2 * q + 1) * HID : (2 * q + 2) * HID]
            dn_out[:, at : at + size] = last[q * HID : (q + 1) * HID]

    for g in range(max(last + 1, 3)):
        if g < 3:
            grads(g)
        if g < last:
            over_z(0, g + 1, back_out)
            over_y(1, g + 1)
    for g in range(last + 1):
        over_z(1, g, front_out)

    def sent(at, sem):
        remote(at, at, sem, sem, core_dev).wait_send()

    for i in (0, 1):
        exchange(i).wait_send()

    @on_middle
    def _():
        sent(xs.at[:, c, pl.ds(0, 5 * FOLD)], zs.at[0])

        @on_core1
        def _():
            sent(xs.at[2, c, pl.ds(0, 5 * FOLD)], zs.at[1])

    @on_end
    def _():
        sent(xs.at[:, c, pl.ds(0, FOLD)], zs.at[0])

        @on_core1
        def _():
            sent(xs.at[2, c, pl.ds(0, FOLD)], zs.at[1])

    sent(xs.at[pl.ds(0, 2), c, pl.ds(0, ZS * FOLD)], ys.at[0])

    @on_core0
    def _():
        sent(xs.at[2, c, pl.ds(0, ZS * FOLD)], ys.at[1])

    @on_core1
    def _():
        sent(xs.at[2, c, pl.ds(0, FOLD)], ys.at[1])

    sent(xs.at[:, c], cs.at[0])
    sent(ms.at[0], xsem.at[0])
    for far in (0, 1):
        m_copy(far, c).wait_send()
    sent(some, ts.at[1])
    tab_y(y).wait_send()
    tab_c(c).wait_send()
    deltas.wait_send()
    for a in range(2):
        sent(pb.at[a, 0], rs.at[a, 0])
        sent(ry.at[a], rs.at[a, 1])
        sent(rz.at[a], rs.at[a, 2])


def place(*refs):
    count = len(refs) // 2
    for i in range(count):
        refs[count + i][...] = refs[i][...]


def local_kernel(
    front_tokens, front_routes, front_mixing, back_tokens, back_routes, back_mixing,
    back_upstream, gate_weight, up_weight, down_weight,
):
    features = front_tokens.shape[2]
    half = features // 2
    quarter = features // 4
    tiles = quarter // LANES
    bf, f32 = jnp.bfloat16, jnp.float32
    vm = pltpu.VMEM
    dma = pltpu.SemaphoreType.DMA
    results = pl.pallas_call(
        functools.partial(kernel, features),
        out_shape=[
            pltpu.VMEM((TOK, features), bf),
            pltpu.VMEM((TOK, features), bf),
            pltpu.VMEM((half, HID), bf),
            pltpu.VMEM((half, HID), bf),
            pltpu.VMEM((HID, half), bf),
        ],
        in_specs=[pl.BlockSpec(memory_space=pltpu.MemorySpace.HBM)] * 10,
        out_specs=[pl.BlockSpec(memory_space=vm)] * 5,
        scratch_shapes=[
            vm((3, TOK, features), bf),
            vm((4, TOP, TOK), jnp.int32),
            vm((features, HID), bf),
            vm((features, HID), bf),
            vm((HID, features), bf),
            vm((3, 2, FOLD, quarter), f32),
            vm((3, FOLD, quarter), bf),
            vm((3, FOLD, quarter), bf),
            vm((3, 2, DEPTH, quarter), bf),
            vm((2, DEPTH, quarter), bf),
            vm((16, LANES), f32),
            vm((BLOCKS, 16, LANES), bf),
            vm((SLOTS, LANES), f32),
            vm((SLOTS, 3 * HID), f32),
            vm((SLOTS, 3 * HID), bf),
            vm((SLOTS, 3 * HID), bf),
            vm((2 * DEPTH, 6 * HID), bf),
            vm((BLOCKS * 16, 2 * HID), f32),
            vm((BLOCKS * 16, 2 * HID), bf),
            vm((BLOCKS * 16, HID), bf),
            vm((2, CS, tiles, DEPTH, LANES), bf),
            vm((2, tiles, DEPTH, LANES), bf),
            vm((2, tiles, ZS * FOLD, LANES), bf),
            vm((2, tiles, ZS * FOLD, LANES), bf),
            vm((2, ZS - 1, tiles, FOLD, LANES), bf),
            vm((tiles, FOLD, LANES), f32),
            dma((10,)), dma((2, 2)),
            dma((2,)), dma((4, 3)), dma((2,)), dma((3, 4)), dma((1,)), dma((17,)),
            dma((1,)), dma((2,)), dma((2,)), dma((2,)), dma((3,)), dma((3,)), dma((2,)),
            dma((2, 3)), dma((2, len(GROUPS), 3)),
        ],
        compiler_params=pltpu.CompilerParams(
            collective_id=0, has_side_effects=True, vmem_limit_bytes=VMEM_LIMIT
        ),
    )(
        back_tokens[0], back_upstream[0], front_tokens[0], back_routes[0].T, back_mixing[0].T,
        front_routes[0].T, front_mixing[0].T, gate_weight[0], up_weight[0], down_weight[0],
    )
    front, back, gate, up, down = pl.pallas_call(
        place,
        out_shape=[jax.ShapeDtypeStruct(item.shape, item.dtype) for item in results],
        in_specs=[pl.BlockSpec(memory_space=vm)] * 5,
        out_specs=[pl.BlockSpec(memory_space=vm)] * 5,
        compiler_params=pltpu.CompilerParams(vmem_limit_bytes=8 * 1024 * 1024),
    )(*results)
    return front[None], back[None], gate[None], up[None], down[None]


def solution(mesh):
    fits = mesh.shape["pipe"] == 2 and mesh.shape["expert"] == BLOCKS
    local = local_kernel if fits else local_collectives
    rows = P("pipe", "expert", None)
    columns = P("pipe", None, "expert")
    return jax.shard_map(
        local,
        mesh=mesh,
        in_specs=(rows,) * 7 + (columns, columns, rows),
        out_specs=(rows, rows, columns, columns, rows),
        check_vma=False,
    )
```

```python
import functools

import jax
import jax.numpy as jnp
from jax import lax
from jax.experimental import pallas as pl
from jax.experimental.pallas import tpu as pltpu
from jax.sharding import PartitionSpec as P

SHARDS = 8
LANES = 128
TOP = 2

weight_unit = 0.0625


def token_weights(routes, mixing):
    hits = routes[:, :, None] == jnp.arange(LANES, dtype=jnp.int32)[None, None, :]
    weights = mixing.astype(jnp.float32) * weight_unit
    return jnp.sum(jnp.where(hits, weights[:, :, None], 0.0), axis=1).astype(jnp.bfloat16)


def rows_dot(rows, matrix, dim):
    return lax.dot_general(
        rows, matrix, (((2,), (dim,)), ((), ())), preferred_element_type=jnp.float32
    )


def grad_dot(rows, deltas):
    return lax.dot_general(
        rows, deltas, (((0, 1), (0, 1)), ((), ())), preferred_element_type=jnp.float32
    ).astype(jnp.bfloat16)


def local_collectives(
    front_tokens,
    front_routes,
    front_mixing,
    back_tokens,
    back_routes,
    back_mixing,
    back_upstream,
    gate_weight,
    up_weight,
    down_weight,
):
    tokens = front_tokens.shape[1]
    features = front_tokens.shape[2]
    gate_cols = gate_weight[0]
    up_cols = up_weight[0]
    down_rows = down_weight[0]
    expert = lax.axis_index("expert") // SHARDS
    picked = (jnp.arange(LANES, dtype=jnp.int32) == expert).astype(jnp.float32)

    front_table = token_weights(front_routes[0], front_mixing[0])
    back_table = token_weights(back_routes[0], back_mixing[0])
    back_load = jnp.concatenate(
        [
            jnp.concatenate([back_tokens[0], jnp.zeros_like(back_table)], axis=1),
            jnp.concatenate([back_upstream[0], back_table], axis=1),
        ],
        axis=0,
    )
    front_load = jnp.concatenate([front_tokens[0], front_table], axis=1)
    back_all = lax.all_gather(back_load, "expert", axis=0)
    front_all = lax.all_gather(front_load, "expert", axis=0)

    def own_weight(table):
        return jnp.sum(table.astype(jnp.float32) * picked, axis=2, keepdims=True)

    back_rows = back_all[:, :tokens, :features]
    upstream = back_all[:, tokens:, :features]
    back_scale = own_weight(back_all[:, tokens:, features:])
    scaled_rows = (upstream.astype(jnp.float32) * back_scale).astype(jnp.bfloat16)
    back_gate = rows_dot(back_rows, gate_cols, 0)
    back_up = rows_dot(back_rows, up_cols, 0)
    hidden_grad = rows_dot(scaled_rows, down_rows, 1)
    gate_sig = jax.nn.sigmoid(back_gate)
    gate_act = back_gate * gate_sig
    back_hidden = (gate_act * back_up).astype(jnp.bfloat16)
    act_slope = gate_sig * (1.0 + back_gate * (1.0 - gate_sig))
    gate_delta = (hidden_grad * back_up * act_slope).astype(jnp.bfloat16)
    up_delta = (hidden_grad * gate_act).astype(jnp.bfloat16)
    sections = jnp.stack(
        [
            grad_dot(back_rows, gate_delta),
            grad_dot(back_rows, up_delta),
            grad_dot(scaled_rows, back_hidden),
        ]
    )
    pipe_count = lax.axis_size("pipe")
    half = features // 2
    upper = lax.axis_index("pipe") * 2 >= pipe_count
    own_start = jnp.where(upper, half, 0)
    own_half = lax.dynamic_slice_in_dim(sections, own_start, half, axis=1)
    leaving = lax.dynamic_slice_in_dim(sections, half - own_start, half, axis=1)
    arrived = lax.ppermute(leaving, "pipe", [(p, pipe_count - 1 - p) for p in range(pipe_count)])

    back_parts = (rows_dot(gate_delta, gate_cols, 1) + rows_dot(up_delta, up_cols, 1)).astype(
        jnp.bfloat16
    )
    front_rows = front_all[:, :, :features]
    front_scale = own_weight(front_all[:, :, features:])
    front_gate = rows_dot(front_rows, gate_cols, 0)
    front_up = rows_dot(front_rows, up_cols, 0)
    front_hidden = (jax.nn.silu(front_gate) * front_up).astype(jnp.bfloat16)
    front_parts = (rows_dot(front_hidden, down_rows, 0) * front_scale).astype(jnp.bfloat16)
    totals = lax.psum_scatter(
        jnp.concatenate([front_parts, back_parts], axis=1), "expert", scatter_dimension=0
    )
    summed = (own_half.astype(jnp.float32) + arrived.astype(jnp.float32)).astype(jnp.bfloat16)
    return (
        totals[:tokens][None],
        totals[tokens:][None],
        summed[0][None],
        summed[1][None],
        summed[2].T[None],
    )


MESH = pl.DeviceIdType.MESH
TOK = 12
EXPERTS = 2
ZS, YS, CS = 4, 2, 2
CHIPS = ZS * YS
BLOCKS = CHIPS * CS
HID = 128
PAIR = 2 * TOK
FOLD = 2 * PAIR
DEPTH = CHIPS * FOLD
SLOTS = CHIPS * PAIR
GROUPS = ((0, 2), (2, 2), (4, 3))
PIECES = ((0, 2), (2, 2), (4, 3))
VMEM_LIMIT = 61 * 1024 * 1024


def nn(a, b):
    return jnp.dot(a, b, preferred_element_type=jnp.float32)


def nt(a, b):
    return lax.dot_general(a, b, (((1,), (1,)), ((), ())), preferred_element_type=jnp.float32)


def tn(a, b):
    return lax.dot_general(a, b, (((0,), (0,)), ((), ())), preferred_element_type=jnp.float32)


def kernel(
    features,
    back_hbm, up_hbm, front_hbm, broutes_hbm, bmix_hbm, froutes_hbm, fmix_hbm, gate_hbm, up_w_hbm, down_hbm,
    front_out, back_out, gate_out, up_out, dn_out,
    stage, mix, gate_w, up_w, down_w, wide, ex_send, ex_recv, xs, ms, tab, tabs, sc, dc, dsend, dm, de,
    r32, drs, ers, pb, rc, ry, zsb, rz, tot,
    local_sems, ex_sems, zs, zr, ys, yr, cs, cr, xsem, xrem, mcs, mcr, ts, tr, dms, rs, rr,
):
    f32, bf = jnp.float32, jnp.bfloat16
    me = lax.axis_index("expert")
    pipe = lax.axis_index("pipe")
    c = me % CS
    y = (me // CS) % YS
    z = me // (CS * YS)
    k = me // SHARDS
    quarter = features // 4
    half = features // 2

    def dev(zz, yy, cc):
        return {"expert": (zz * YS + yy) * CS + cc}

    zpeer = [None] + [(z + d) % ZS for d in range(1, ZS)]
    zfrom = [None] + [(z + ZS - d) % ZS for d in range(1, ZS)]
    core_dev = dev(z, y, 1 - c)
    y_dev = dev(z, 1 - y, c)
    z_dev = [None] + [dev(zpeer[d], y, c) for d in range(1, ZS)]
    mirror = {"pipe": 1 - pipe}
    low = z < 2
    inner = jnp.where(low, z, 3 - z)

    def real(s):
        return jnp.where(low, s, 3 - s)

    sources = [z, real(1 - inner), real(2), real(3)]
    z_in = dev(real(1 + inner), y, c)
    z_out = dev(real(0), y, c)

    loads = [
        pltpu.make_async_copy(src, dst, local_sems.at[i])
        for i, (src, dst) in enumerate(
            [
                (back_hbm, stage.at[0]), (up_hbm, stage.at[1]), (front_hbm, stage.at[2]),
                (froutes_hbm, mix.at[0]), (fmix_hbm, mix.at[1]), (broutes_hbm, mix.at[2]), (bmix_hbm, mix.at[3]),
                (gate_hbm, gate_w), (up_w_hbm, up_w), (down_hbm, down_w),
            ]
        )
    ]
    for load in loads:
        load.start()

    barrier = pltpu.get_barrier_semaphore()
    for target in [core_dev, y_dev, z_dev[1], z_dev[2], z_dev[3], mirror]:
        pl.semaphore_signal(barrier, inc=1, device_id=target, device_id_type=MESH)

    lanes = lax.broadcasted_iota(jnp.int32, (TOK, LANES), 1)
    square = (TOK, TOK)
    diagonal = lax.broadcasted_iota(jnp.int32, square, 0) == lax.broadcasted_iota(jnp.int32, square, 1)

    def upright(row):
        wide_row = jnp.broadcast_to(row.astype(f32), square)
        return jnp.sum(jnp.where(diagonal, wide_row, 0.0), axis=1, keepdims=True)

    def table(routes, mixing, base):
        out = jnp.zeros((TOK, LANES), f32)
        for j in range(TOP):
            weight = upright(mixing[j : j + 1]) * weight_unit
            out = out + jnp.where(upright(routes[j : j + 1]).astype(jnp.int32) + base == lanes, weight, 0.0)
        return out

    chip = y * ZS + z
    own_tab = c * CHIPS + chip

    for load in loads[:7]:
        load.wait()
    for a in range(3):
        rows = stage[a].astype(f32)
        for h in range(2):
            for q in range(2):
                at = (2 * h + q) * quarter
                piece = rows[:, at : at + quarter]
                for cc in range(2):
                    top = q * PAIR + cc * TOK
                    wide[a, h, top : top + TOK, :] = jnp.where(c == cc, piece, 0.0)
    for a in range(3):
        ex_send[a] = wide[a, 1 - c].astype(bf)
    tab[...] = jnp.zeros_like(tab)
    tab[0:TOK, :] = table(mix[2], mix[3], 0) + table(mix[0], mix[1], EXPERTS)
    tabs[own_tab] = tab[...].astype(bf)
    pl.semaphore_wait(barrier, 6)

    def remote(src, dst, ssem, rsem, target):
        return pltpu.make_async_remote_copy(
            src_ref=src, dst_ref=dst, send_sem=ssem, recv_sem=rsem,
            device_id=target, device_id_type=MESH,
        )

    def exchange(i):
        part = pl.ds(0, 2) if i == 0 else pl.ds(2, 1)
        return remote(ex_send.at[part], ex_recv.at[part], ex_sems.at[0, i], ex_sems.at[1, i], core_dev)

    exchange(0).start()
    exchange(1).start()

    def tab_z(d):
        return remote(tabs.at[own_tab], tabs.at[own_tab], ts.at[1], tr.at[1], z_dev[d])

    some = tabs.at[pl.ds(0, ZS - 1)]
    three_tabs = remote(some, some, ts.at[1], tr.at[1], z_dev[1])

    def tab_y(yy):
        part = tabs.at[pl.ds(c * CHIPS + yy * ZS, ZS)]
        return remote(part, part, ts.at[0], tr.at[0], y_dev)

    def tab_c(cc):
        part = tabs.at[pl.ds(cc * CHIPS, CHIPS)]
        return remote(part, part, ts.at[2], tr.at[2], core_dev)

    for d in (1, 2, 3):
        tab_z(d).start()

    def rows_of(zz, yy):
        return pl.ds(pl.multiple_of((yy * ZS + zz) * FOLD, 16), FOLD)

    def block(a, h, zz, yy):
        return xs.at[a, h, rows_of(zz, yy)]

    def z_copy(a, slot, far=0):
        yy = 1 - y if far else y
        own_at = block(a, c, z, yy)
        if slot == 0:
            return remote(own_at, own_at, zs.at[far], zr.at[a + far, inner], z_in)
        if slot == 1:
            return remote(own_at, own_at, zs.at[far], zr.at[a + far, 0], z_out)
        i = slot - 1
        at = block(a, c, sources[i], yy)
        target, arrival = (z_in, 2) if i == 1 else (z_out, i - 1)
        return remote(at, at, zs.at[far], zr.at[a + far, arrival], target)

    def z_arrival(a, i, far=0):
        at = block(a, c, sources[i], 1 - y if far else y)
        return remote(at, at, zs.at[far], zr.at[a + far, i - 1], z_in)

    def y_copy(a, i, yy):
        at = block(a, c, sources[i], yy)
        return remote(at, at, ys.at[a // 2], yr.at[a, i], y_dev)

    def c_copy(a, i, far, cc):
        at = block(a, cc, sources[i], 1 - y if far else y)
        return remote(at, at, cs.at[0], cr.at[4 * far + i if a < 2 else 8], core_dev)

    def x_copy(i, far):
        rows = rows_of(sources[i], 1 - y if far else y)
        return remote(xs.at[c, 1 - pipe, rows], ms.at[c, rows], xsem.at[0], xrem.at[far], mirror)

    def x_group(far):
        yy = 1 - y if far else y
        rows = pl.ds(pl.multiple_of(yy * ZS * FOLD, 16), ZS * FOLD)
        return remote(xs.at[c, 1 - pipe, rows], ms.at[c, rows], xsem.at[0], xrem.at[far], mirror)

    def m_copy(far, cc):
        yy = 1 - y if far else y
        rows = pl.ds(pl.multiple_of(yy * ZS * FOLD, 16), ZS * FOLD)
        return remote(ms.at[cc, rows], ms.at[cc, rows], mcs.at[far], mcr.at[far], core_dev)

    def own(a):
        xs[a, c, rows_of(z, y), :] = (wide[a, c] + ex_recv[a].astype(f32)).astype(bf)

    def z_begin(a, far=0):
        z_copy(a, 0, far).start()

        @pl.when(inner == 1)
        def _():
            z_copy(a, 1, far).start()

    def z_arrive(a, i, far=0):
        z_arrival(a, i, far).wait_recv()

        @pl.when(inner == 1)
        def _():
            z_copy(a, i + 1, far).start()

    def y_go(a, i):
        y_copy(a, i, y).start()

    def c_go(a, i, far=0):
        c_copy(a, i, far, c).start()

    def y_arrive(a, i):
        y_copy(a, i, 1 - y).wait_recv()
        c_copy(a, i, 1, c).start()

    def mirror_go(i, far):
        pair = xs.at[pl.ds(0, 2), 1 - c, rows_of(sources[i], 1 - y if far else y)]
        remote(pair, pair, cs.at[0], cr.at[4 * far + i], core_dev).wait_recv()
        x_copy(i, far).start()

    def near(a, i):
        z_arrival(a, i).wait_recv()
        c_go(a, i)

    def pass_on(a, i):
        z_arrival(a, i).wait_recv()
        z_copy(a, i + 1).start()
        c_go(a, i)

    def peer_near(i):
        z_arrival(2, i, 1).wait_recv()
        c_go(2, i, 1)

    def peer_pass_on(i):
        z_arrival(2, i, 1).wait_recv()
        z_copy(2, i + 1, 1).start()
        c_go(2, i, 1)

    def tabs_over_y():
        three_tabs.wait_recv()
        tab_y(y).start()

    def tabs_over_cores():
        tab_y(1 - y).wait_recv()
        tab_c(c).start()

    def peer_begin():
        y_arrive(2, 0)
        z_copy(2, 0, 1).start()

    on_core0 = pl.when(c == 0)
    on_core1 = pl.when(c == 1)
    on_end = pl.when(inner == 0)
    on_middle = pl.when(inner == 1)

    exchange(0).wait_recv()
    for a in (0, 1):
        own(a)
        z_begin(a)
        y_go(a, 0)
        c_go(a, 0)
    exchange(1).wait_recv()
    own(2)
    c_go(2, 0)

    @on_core1
    def _():
        y_go(2, 0)

    @on_middle
    def _():
        pass_on(0, 1)
        y_go(0, 1)
        pass_on(0, 2)
        y_go(0, 2)
        tabs_over_y()
        pass_on(1, 1)
        y_go(1, 1)
        pass_on(1, 2)
        y_go(1, 2)
        z_copy(2, 0).start()
        y_arrive(0, 0)
        y_arrive(1, 0)

        @on_core1
        def _():
            peer_begin()

        pass_on(0, 3)
        y_go(0, 3)
        pass_on(2, 1)

        @on_core1
        def _():
            peer_pass_on(1)

        pass_on(1, 3)
        y_go(1, 3)
        z_copy(2, 1).start()

        @on_core0
        def _():
            y_go(2, 0)
            y_go(2, 1)

        @on_core1
        def _():
            z_copy(2, 1, 1).start()

        mirror_go(0, 0)
        pass_on(2, 2)

        @on_core0
        def _():
            y_go(2, 2)

        @on_core1
        def _():
            peer_pass_on(2)

        mirror_go(1, 0)
        tabs_over_cores()
        y_arrive(0, 1)
        pass_on(2, 3)

        @on_core0
        def _():
            y_go(2, 3)

        @on_core1
        def _():
            peer_pass_on(3)

        mirror_go(0, 1)
        y_arrive(1, 1)
        mirror_go(2, 0)
        y_arrive(0, 2)
        mirror_go(1, 1)
        y_arrive(1, 2)
        mirror_go(3, 0)

    @on_end
    def _():
        z_copy(2, 0).start()
        near(0, 1)
        y_go(0, 1)
        tabs_over_y()
        near(1, 1)
        y_go(1, 1)
        y_arrive(0, 0)
        y_arrive(1, 0)

        @on_core1
        def _():
            peer_begin()

        mirror_go(0, 0)
        near(0, 2)
        y_go(0, 2)
        near(1, 2)
        y_go(1, 2)
        mirror_go(1, 0)
        tabs_over_cores()
        y_arrive(0, 1)
        near(0, 3)
        y_go(0, 3)
        mirror_go(0, 1)
        y_arrive(1, 1)
        near(1, 3)
        y_go(1, 3)

        @on_core0
        def _():
            y_go(2, 0)

        mirror_go(2, 0)
        y_arrive(0, 2)
        mirror_go(1, 1)
        near(2, 1)

        @on_core0
        def _():
            y_go(2, 1)

        @on_core1
        def _():
            peer_near(1)

        y_arrive(1, 2)
        mirror_go(3, 0)

    for load in loads[7:]:
        load.wait()
    tab_c(1 - c).wait_recv()
    for b in range(CHIPS):
        for cc in range(CS):
            at = b * PAIR + cc * TOK
            tab[...] = tabs[cc * CHIPS + b].astype(f32)
            sc[at : at + TOK, :] = tab[0:TOK, :]
    for a in (0, 1):
        y_arrive(a, 3)
    mirror_go(2, 1)
    mirror_go(3, 1)

    def front_step(i):
        if i in (0, 2):
            @on_end
            def _():
                near(2, 2 + i // 2)

                @on_core0
                def _():
                    y_go(2, 2 + i // 2)

                @on_core1
                def _():
                    peer_near(2 + i // 2)

        @on_core0
        def _():
            y_arrive(2, i)

    slot_lanes = lax.broadcasted_iota(jnp.int32, (SLOTS, LANES), 1)

    def scale_of(base):
        return jnp.sum(jnp.where(slot_lanes == k + base, sc[...], 0.0), axis=1, keepdims=True)

    def hidden(a):
        total = None
        for h in range(2):
            parts = []
            for q in range(2):
                at = (2 * h + q) * quarter
                parts += [gate_w[at : at + quarter, :], up_w[at : at + quarter, :]]
            term = nn(xs[a, h], jnp.concatenate(parts, axis=1))
            total = term if total is None else total + term
        total = total.reshape(CHIPS, FOLD, 4 * HID)
        both = total[:, 0:PAIR, 0 : 2 * HID] + total[:, PAIR:, 2 * HID :]
        both = both.reshape(SLOTS, 2 * HID)
        return both[:, 0:HID], both[:, HID:]

    gate, up = hidden(0)
    front_step(0)
    total = None
    for h in range(2):
        at = 2 * h * quarter
        pair = jnp.concatenate(
            [down_w[:, at : at + quarter], down_w[:, at + quarter : at + 2 * quarter]], axis=0
        )
        term = nt(xs[1, h], pair)
        total = term if total is None else total + term
    total = total.reshape(CHIPS, FOLD, 2 * HID)
    scale = scale_of(0)
    grad = (total[:, 0:PAIR, 0:HID] + total[:, PAIR:, HID:]).reshape(SLOTS, HID) * scale
    sig = 1.0 / (1.0 + jnp.exp(-gate))
    act = gate * sig
    dc[:, 0:HID] = grad * up * (sig * (1.0 + gate * (1.0 - sig)))
    dc[:, HID : 2 * HID] = grad * act
    dc[:, 2 * HID :] = act * up * scale
    dsend[...] = dc[...].astype(bf)
    deltas = remote(dsend, dm, dms.at[0], dms.at[1], mirror)
    deltas.start()

    def by_device(width):
        for b in range(CHIPS):
            for cc in range(CS):
                at = b * PAIR + cc * TOK
                to = cc * CHIPS * 16 + b * 16
                r32[to : to + TOK, 0:width] = dc[at : at + TOK, 0:width]
                r32[to + TOK : to + 16, 0:width] = dc[at + 8 : at + TOK, 0:width]
        return r32[:, 0:width].astype(bf)

    drs[...] = by_device(2 * HID)

    def core_sum(a, g):
        j, n = GROUPS[g]
        part = pl.ds(j, n)
        return remote(pb.at[a, 1 - c, part], rc.at[a, part], rs.at[a, 0], rr.at[a, g, 0], core_dev)

    def y_sum(a, g):
        j, n = GROUPS[g]
        part = pl.ds(j, n)
        rows = pl.ds(pl.multiple_of((1 - y) * ZS * FOLD, 16), ZS * FOLD)
        return remote(pb.at[a, c, part, rows], ry.at[a, part], rs.at[a, 1], rr.at[a, g, 1], y_dev)

    def z_sum(a, g, d):
        j, n = GROUPS[g]
        part = pl.ds(j, n)
        rows = pl.ds(pl.multiple_of(zpeer[d] * FOLD, 16), FOLD)
        return remote(zsb.at[a, part, rows], rz.at[a, d - 1, part], rs.at[a, 2], rr.at[a, g, 2], z_dev[d])

    early = lax.broadcasted_iota(jnp.int32, (1, 1, 8, 1), 2) < 4

    def part(a, g):
        j, n = GROUPS[g]
        wide_of = n * LANES
        outs = []
        for q in range(4):
            at = q * quarter + j * LANES
            if a == 0:
                both = jnp.concatenate([gate_w[at : at + wide_of, :], up_w[at : at + wide_of, :]], axis=1)
                out = nt(drs[...], both)
            else:
                out = nn(ers[...], down_w[:, at : at + wide_of])
            outs.append(out.reshape(CS, CHIPS, 16, wide_of))
        tops = [out[:, :, 0:8] for out in outs]
        ends = [jnp.where(early, outs[2 * i][:, :, 8:16], outs[2 * i + 1][:, :, 8:16]) for i in range(2)]
        folded = jnp.concatenate(tops + ends, axis=2).reshape(CS, DEPTH, wide_of).astype(bf)
        for i in range(n):
            pb[a, :, j + i] = folded[:, :, i * LANES : (i + 1) * LANES]
        core_sum(a, g).start()

    def over_cores(a, g):
        j, n = GROUPS[g]
        part = pl.ds(j, n)
        core_sum(a, g).wait_recv()
        for yy in (1 - y, y):
            rows = pl.ds(pl.multiple_of(yy * ZS * FOLD, 16), ZS * FOLD)
            pb[a, c, part, rows, :] = (
                pb[a, c, part, rows, :].astype(f32) + rc[a, part, rows, :].astype(f32)
            ).astype(bf)
            if yy is not y:
                y_sum(a, g).start()

    def over_y(a, g):
        j, n = GROUPS[g]
        part = pl.ds(j, n)
        y_sum(a, g).wait_recv()
        rows = pl.ds(pl.multiple_of(y * ZS * FOLD, 16), ZS * FOLD)
        zsb[a, part] = (pb[a, c, part, rows, :].astype(f32) + ry[a, part].astype(f32)).astype(bf)
        for d in (1, 2, 3):
            z_sum(a, g, d).start()

    def over_z(a, g, out):
        j, n = GROUPS[g]
        part = pl.ds(j, n)
        rows = pl.ds(pl.multiple_of(z * FOLD, 16), FOLD)
        arrived = rz.at[a, :, part]
        remote(arrived, arrived, rs.at[a, 2], rr.at[a, g, 2], y_dev).wait_recv()
        total = zsb[a, part, rows, :].astype(f32)
        for d in (1, 2, 3):
            total = total + rz[a, d - 1, part].astype(f32)
        tot[part] = total
        for i in range(n):
            for q in range(4):
                piece = jnp.concatenate(
                    [tot[j + i, 8 * q : 8 * q + 8], tot[j + i, 32 + 4 * q : 36 + 4 * q]], axis=0
                )
                at = q * quarter + (j + i) * LANES
                out[:, at : at + LANES] = piece.astype(bf)

    last = len(GROUPS) - 1
    for g in range(last + 1):
        part(0, g)
        if g < 3:
            front_step(g + 1)
        if g:
            over_cores(0, g - 1)
    for g in range(last + 1, 3):
        front_step(g + 1)
    over_cores(0, last)
    every = xs.at[2, 1 - c]
    remote(every, every, cs.at[0], cr.at[8], core_dev).wait_recv()
    gate, up = hidden(2)
    dc[:, 0:HID] = gate / (1.0 + jnp.exp(-gate)) * up * scale_of(EXPERTS)
    ers[...] = by_device(HID)
    for g in range(last + 1):
        part(1, g)
        if g:
            over_cores(1, g - 1)
        over_y(0, g)
    over_cores(1, last)
    for far in (0, 1):
        x_group(far).wait_recv()
        m_copy(far, c).start()
    over_z(0, 0, back_out)
    deltas.wait_recv()

    def spread(rows):
        rows = rows.reshape(CHIPS, PAIR, 3 * HID)
        pair, last = rows[:, :, 0 : 2 * HID], rows[:, :, 2 * HID :]
        empty, short = jnp.zeros_like(pair), jnp.zeros_like(last)
        first = jnp.concatenate([pair, empty, last, short], axis=2)
        second = jnp.concatenate([empty, pair, short, last], axis=2)
        return jnp.concatenate([first, second], axis=1).reshape(DEPTH, 6 * HID).astype(bf)

    de[0:DEPTH, :] = spread(dsend[...].astype(f32))
    de[DEPTH:, :] = spread(dm[...].astype(f32))
    over_y(1, 0)
    for far in (0, 1):
        m_copy(far, 1 - c).wait_recv()

    def grads(g):
        j, n = PIECES[g]
        cols = slice(j * LANES, (j + n) * LANES)
        size = n * LANES
        both = tn(jnp.concatenate([xs[0, pipe, :, cols], ms[0, :, cols]], axis=0), de[:, 0 : 4 * HID]).astype(bf)
        last = tn(de[:, 4 * HID :], jnp.concatenate([xs[1, pipe, :, cols], ms[1, :, cols]], axis=0)).astype(bf)
        for q in range(2):
            at = q * quarter + j * LANES
            gate_out[at : at + size, :] = both[:, 2 * q * HID : (2 * q + 1) * HID]
            up_out[at : at + size, :] = both[:, (2 * q + 1) * HID : (2 * q + 2) * HID]
            dn_out[:, at : at + size] = last[q * HID : (q + 1) * HID]

    for g in range(max(last + 1, 3)):
        if g < 3:
            grads(g)
        if g < last:
            over_y(1, g + 1)
    for g in range(1, last + 1):
        over_z(0, g, back_out)
    for g in range(last + 1):
        over_z(1, g, front_out)

    def sent(at, sem):
        remote(at, at, sem, sem, core_dev).wait_send()

    for i in (0, 1):
        exchange(i).wait_send()

    @on_middle
    def _():
        sent(xs.at[:, c, pl.ds(0, 5 * FOLD)], zs.at[0])

        @on_core1
        def _():
            sent(xs.at[2, c, pl.ds(0, 5 * FOLD)], zs.at[1])

    @on_end
    def _():
        sent(xs.at[:, c, pl.ds(0, FOLD)], zs.at[0])

        @on_core1
        def _():
            sent(xs.at[2, c, pl.ds(0, FOLD)], zs.at[1])

    sent(xs.at[pl.ds(0, 2), c, pl.ds(0, ZS * FOLD)], ys.at[0])

    @on_core0
    def _():
        sent(xs.at[2, c, pl.ds(0, ZS * FOLD)], ys.at[1])

    @on_core1
    def _():
        sent(xs.at[2, c, pl.ds(0, FOLD)], ys.at[1])

    sent(xs.at[:, c], cs.at[0])
    sent(ms.at[0], xsem.at[0])
    for far in (0, 1):
        m_copy(far, c).wait_send()
    sent(some, ts.at[1])
    tab_y(y).wait_send()
    tab_c(c).wait_send()
    deltas.wait_send()
    for a in range(2):
        sent(pb.at[a, 0], rs.at[a, 0])
        sent(ry.at[a], rs.at[a, 1])
        sent(rz.at[a], rs.at[a, 2])


def place(*refs):
    count = len(refs) // 2
    for i in range(count):
        refs[count + i][...] = refs[i][...]


def local_kernel(
    front_tokens, front_routes, front_mixing, back_tokens, back_routes, back_mixing,
    back_upstream, gate_weight, up_weight, down_weight,
):
    features = front_tokens.shape[2]
    half = features // 2
    quarter = features // 4
    tiles = quarter // LANES
    bf, f32 = jnp.bfloat16, jnp.float32
    vm = pltpu.VMEM
    dma = pltpu.SemaphoreType.DMA
    results = pl.pallas_call(
        functools.partial(kernel, features),
        out_shape=[
            pltpu.VMEM((TOK, features), bf),
            pltpu.VMEM((TOK, features), bf),
            pltpu.VMEM((half, HID), bf),
            pltpu.VMEM((half, HID), bf),
            pltpu.VMEM((HID, half), bf),
        ],
        in_specs=[pl.BlockSpec(memory_space=pltpu.MemorySpace.HBM)] * 10,
        out_specs=[pl.BlockSpec(memory_space=vm)] * 5,
        scratch_shapes=[
            vm((3, TOK, features), bf),
            vm((4, TOP, TOK), jnp.int32),
            vm((features, HID), bf),
            vm((features, HID), bf),
            vm((HID, features), bf),
            vm((3, 2, FOLD, quarter), f32),
            vm((3, FOLD, quarter), bf),
            vm((3, FOLD, quarter), bf),
            vm((3, 2, DEPTH, quarter), bf),
            vm((2, DEPTH, quarter), bf),
            vm((16, LANES), f32),
            vm((BLOCKS, 16, LANES), bf),
            vm((SLOTS, LANES), f32),
            vm((SLOTS, 3 * HID), f32),
            vm((SLOTS, 3 * HID), bf),
            vm((SLOTS, 3 * HID), bf),
            vm((2 * DEPTH, 6 * HID), bf),
            vm((BLOCKS * 16, 2 * HID), f32),
            vm((BLOCKS * 16, 2 * HID), bf),
            vm((BLOCKS * 16, HID), bf),
            vm((2, CS, tiles, DEPTH, LANES), bf),
            vm((2, tiles, DEPTH, LANES), bf),
            vm((2, tiles, ZS * FOLD, LANES), bf),
            vm((2, tiles, ZS * FOLD, LANES), bf),
            vm((2, ZS - 1, tiles, FOLD, LANES), bf),
            vm((tiles, FOLD, LANES), f32),
            dma((10,)), dma((2, 2)),
            dma((2,)), dma((4, 3)), dma((2,)), dma((3, 4)), dma((1,)), dma((9,)),
            dma((1,)), dma((2,)), dma((2,)), dma((2,)), dma((3,)), dma((3,)), dma((2,)),
            dma((2, 3)), dma((2, len(GROUPS), 3)),
        ],
        compiler_params=pltpu.CompilerParams(
            collective_id=0, has_side_effects=True, vmem_limit_bytes=VMEM_LIMIT
        ),
    )(
        back_tokens[0], back_upstream[0], front_tokens[0], back_routes[0].T, back_mixing[0].T,
        front_routes[0].T, front_mixing[0].T, gate_weight[0], up_weight[0], down_weight[0],
    )
    front, back, gate, up, down = pl.pallas_call(
        place,
        out_shape=[jax.ShapeDtypeStruct(item.shape, item.dtype) for item in results],
        in_specs=[pl.BlockSpec(memory_space=vm)] * 5,
        out_specs=[pl.BlockSpec(memory_space=vm)] * 5,
        compiler_params=pltpu.CompilerParams(vmem_limit_bytes=8 * 1024 * 1024),
    )(*results)
    return front[None], back[None], gate[None], up[None], down[None]


def solution(mesh):
    fits = mesh.shape["pipe"] == 2 and mesh.shape["expert"] == BLOCKS
    local = local_kernel if fits else local_collectives
    rows = P("pipe", "expert", None)
    columns = P("pipe", None, "expert")
    return jax.shard_map(
        local,
        mesh=mesh,
        in_specs=(rows,) * 7 + (columns, columns, rows),
        out_specs=(rows, rows, columns, columns, rows),
        check_vma=False,
    )
```
